512 devices in a mesh: ep: 128 (over x, y_lo, z), dp: 4 (over y_hi, core).
Axes of the slice: x: 4, y: 4 (y_hi: 2, y_lo: 2; y = y_hi * 2 + y_lo), z: 16, core: 2. Of those that a mesh axis runs over, the one named last changes fastest.
Arguments:
- tokens: bfloat16 [65536, 2048], P(('ep', 'dp')), may hold values from -6 to 6
- cotangent: bfloat16 [65536, 2048], P(('ep', 'dp')), may hold values from -6 to 6
- experts: int32 [65536, 2], P(('ep', 'dp')), may hold values from 0 to 127, all different within a row; in each aligned block of 128 rows (0 to 127, 128 to 255, ...) at most 3 rows name the same one
- gates: float32 [65536, 2], P(('ep', 'dp')), may hold values from 0.2 to 1
- weights: bfloat16 [128, 3, 2048, 384], P('ep', None, 'dp'), may hold values from -0.1875 to 0.1875
- swap_flags: int32 [64], replicated, may hold values from 0 to 1, as said below
Outputs:
- outputs: bfloat16 [65536, 2048], P(('ep', 'dp'))
- input_grads: bfloat16 [65536, 2048], P(('ep', 'dp'))
- expert_grads: bfloat16 [128, 3, 2048, 384], P('ep', None, 'dp')
The draws below stay inside these ranges and needn't reach their ends.
Inputs may be any that keep to these rules, and one draw needn't show every extreme that they name: `experts`: in each aligned block of 128 rows (the rows of one device) no expert is named more than 3 times; the two ids of a row differ. `swap_flags`: exactly 16 entries are 1.
All inputs are finite; a program needn't handle non-finite values.
Results may differ from the reference program's by a relative error of at most 0.012.
Values may be sent and summed in bfloat16 or wider, within the bound.
No kernel may reach another device: no remote copies, remote signals or barrier semaphores. Data moves between devices by JAX's collectives and lax.ppermute only.
A program may use at most 64 MiB of HBM per device.

```python
import math
import jax
import jax.numpy as jnp
import numpy as np
from jax import lax

D = 2048
FW = 384
TOP = 2
TOK_DEV = 128
EXPERTS = 128
HALF = 64
PAIRS = 16
CAP = 3
TOKENS = 65536
N_EP = 128
N_DP = 4


def draw_swap_flags(key, part):
    own_key = jax.random.fold_in(key, 9173)
    scores = jax.random.randint(own_key, (HALF,), 0, 1 << 20) * HALF + jnp.arange(HALF, dtype=jnp.int32)
    order = jnp.argsort(jnp.argsort(scores, stable=True), stable=True)
    return (order < PAIRS).astype(jnp.int32)


def level_of(rng, extent, cuts, low, high):
    factor_of = 1.0
    for axis_at, blocks in cuts:
        steps = jax.random.uniform(jax.random.fold_in(jax.random.fold_in(rng, 6), axis_at), (blocks,), jnp.float32, low / len(cuts), high / len(cuts))
        factor_of = factor_of * jnp.repeat(jnp.exp(steps), extent[axis_at] // blocks).reshape((-1,) + (1,) * (len(extent) - 1 - axis_at))
    return factor_of


def assign_block(stream_key, own, number, rows, number_of, top, most, skew):
    ranking = jax.random.permutation(stream_key, number_of)
    packed, common = portions_of(number_of, rows * top, most, skew, True), portions_of(number_of, rows * top, most, skew, False)
    places = jnp.arange(number_of)

    def named(lengths, turn):
        used = int((lengths > 0).sum())
        fixed = max(1, used // 4)
        moved = fixed + (places - fixed + turn * (used - fixed)) % max(1, number_of - fixed)
        return jnp.zeros((number_of,), jnp.int32).at[ranking[jnp.where(places < fixed, places, moved)]].set(jnp.asarray(lengths, jnp.int32))

    lengths = jnp.where(number % 4 == 0, named(packed, number // 4), named(common, number - number // 4 - 1))
    mixed = jax.random.permutation(jax.random.fold_in(own, 3), number_of)
    giver, receiver = mixed[0:number_of // 2 * 2:2], mixed[1:number_of // 2 * 2:2]
    slack = jnp.minimum(lengths[giver] - 1, most - lengths[receiver]) // 2
    slack = jnp.where((giver == ranking[0]) | (receiver == ranking[0]) | (lengths[receiver] == 0), 0, jnp.maximum(slack, 0))
    moved = jax.random.randint(jax.random.fold_in(own, 4), (number_of // 2,), 0, 1 << 20) % (slack + 1)
    lengths = lengths.at[giver].add(-moved).at[receiver].add(moved)
    items = jnp.searchsorted(jnp.cumsum(lengths), jnp.arange(rows * top), side="right").astype(jnp.int32)
    listing = items.reshape(top, rows).T
    listing = listing[jax.random.permutation(jax.random.fold_in(own, 1), rows)]
    turn = jax.random.randint(jax.random.fold_in(own, 2), (rows, 1), 0, top)
    return jnp.take_along_axis(listing, (jnp.arange(top)[None, :] + turn) % top, axis=1)


def portions_of(number_of, total, bound, slope, full):
    portions = [(1 << 20) // math.isqrt(grade ** slope) + 1 for grade in range(1, number_of + 1)]
    largest = bound if full else min(bound, max(-(-total // number_of), total * portions[0] // sum(portions)))
    least = 1 if total - largest >= number_of - 1 else 0
    given, rest = [largest] + [least] * (number_of - 1), total - largest - least * (number_of - 1)
    while rest > 0:
        free = [i for i in range(1, number_of) if given[i] < largest] or [i for i in range(1, number_of) if given[i] < bound]
        whole, left = sum([portions[i] for i in free]), rest
        for i in free:
            extra = min(bound - given[i], max(1, left * portions[i] // whole), rest)
            given[i] = given[i] + extra
            rest = rest - extra
    return np.array(given)


def gaussian(rng, dims, spread, limit, shards=(), held_as=jnp.bfloat16):
    array = spread * jax.random.normal(rng, dims, jnp.float32)
    if shards:
        array = array * level_of(rng, dims, shards, -0.22, 0.18)
    return jnp.clip(array, -limit, limit).astype(held_as)


def setup_inputs(seed: int = 0) -> dict:
    arg_keys = jax.random.split(jax.random.key(seed), 7)
    tokens = gaussian(arg_keys[0], (TOKENS, D), 1.0, 6.0, ((0, 512),))
    cotangent = gaussian(arg_keys[1], (TOKENS, D), 1.0, 6.0, ((0, 512),))
    experts_keys = jax.random.split(jax.random.fold_in(arg_keys[2], 1), TOKENS // TOK_DEV)
    experts_turns = jax.random.permutation(jax.random.fold_in(arg_keys[2], 3), TOKENS // TOK_DEV)
    experts = jax.vmap(lambda own, number: assign_block(jax.random.fold_in(arg_keys[2], 2), own, number, TOK_DEV, EXPERTS, TOP, CAP, 2))(experts_keys, experts_turns).reshape((TOKENS, TOP))
    gates = jnp.clip(jnp.exp(math.log(1.0) - 1.609438 * jax.random.uniform(arg_keys[3], (TOKENS, TOP), jnp.float32) ** level_of(arg_keys[3], (TOKENS, TOP), ((0, 512),), -0.2, 0.2)), 0.2, 1.0)
    weights = gaussian(arg_keys[4], (EXPERTS, 3, D, FW), (D // 2) ** -0.5, 0.1875, ((0, 128), (2, 4)))
    swap_flags = draw_swap_flags(jax.random.fold_in(arg_keys[6], 71), 0)
    return dict(tokens=tokens, cotangent=cotangent, experts=experts, gates=gates, weights=weights, swap_flags=swap_flags)


def reference(tokens, cotangent, experts, gates, weights, swap_flags):
    route_total = TOKENS * TOP
    token_of = jnp.arange(route_total, dtype=jnp.int32) // TOP
    replica_of = (token_of // TOK_DEV) % N_DP
    routed = experts.reshape(-1)
    gate_flat = gates.reshape(-1)
    cap_rows = CAP * N_EP

    def per_expert(carry, expert):
        out_rows, grad_rows = carry
        stacked = lax.dynamic_index_in_dim(weights, expert, 0, keepdims=False)
        w_gate, w_up, w_down = stacked[0], stacked[1], stacked[2]
        summed = jnp.zeros((3, D, FW), jnp.float32)
        for replica in range(N_DP):
            chosen = (routed == expert) & (replica_of == replica)
            picked = jnp.nonzero(chosen, size=cap_rows, fill_value=route_total)[0].astype(jnp.int32)
            live = picked < route_total
            safe_pick = jnp.minimum(picked, route_total - 1)
            source = token_of[safe_pick]
            rows_x = jnp.where(live[:, None], tokens[source], jnp.zeros((), tokens.dtype))
            weight_col = jnp.where(live, gate_flat[safe_pick], jnp.zeros((), gate_flat.dtype))
            rows_dy = (weight_col[:, None] * cotangent[source].astype(jnp.float32)).astype(jnp.bfloat16)
            pre_gate = jnp.dot(rows_x, w_gate, preferred_element_type=jnp.float32)
            pre_up = jnp.dot(rows_x, w_up, preferred_element_type=jnp.float32)
            gate_sig = jax.nn.sigmoid(pre_gate)
            gate_act = pre_gate * gate_sig
            hidden = (gate_act * pre_up).astype(jnp.bfloat16)
            expert_out = jnp.dot(hidden, w_down.T, preferred_element_type=jnp.float32).astype(jnp.bfloat16)
            hidden_grad = jnp.dot(rows_dy, w_down, preferred_element_type=jnp.float32)
            gate_pre = (hidden_grad * pre_up * gate_sig * (1.0 + pre_gate * (1.0 - gate_sig))).astype(jnp.bfloat16)
            up_pre = (hidden_grad * gate_act).astype(jnp.bfloat16)
            in_grad = (jnp.dot(gate_pre, w_gate.T, preferred_element_type=jnp.float32)
                       + jnp.dot(up_pre, w_up.T, preferred_element_type=jnp.float32)).astype(jnp.bfloat16)
            gate_part = jnp.dot(rows_x.T, gate_pre, preferred_element_type=jnp.float32).astype(jnp.bfloat16)
            up_part = jnp.dot(rows_x.T, up_pre, preferred_element_type=jnp.float32).astype(jnp.bfloat16)
            down_part = jnp.dot(rows_dy.T, hidden, preferred_element_type=jnp.float32).astype(jnp.bfloat16)
            summed = summed + jnp.stack([gate_part, up_part, down_part]).astype(jnp.float32)
            out_rows = out_rows.at[picked].set(expert_out)
            grad_rows = grad_rows.at[picked].set(in_grad)
        return (out_rows, grad_rows), summed.astype(jnp.bfloat16)

    blank = jnp.zeros((route_total + 1, D), jnp.bfloat16)
    (out_rows, grad_rows), per_grads = lax.scan(per_expert, (blank, blank), jnp.arange(EXPERTS, dtype=jnp.int32))
    owners = jnp.arange(N_EP, dtype=jnp.int32)
    half_ep = N_EP // 2
    flag_of = swap_flags[owners % half_ep] > 0
    held = jnp.where(flag_of, (owners + half_ep) % N_EP, owners).astype(jnp.int32)
    expert_grads = per_grads[held]
    per_route = out_rows[:route_total].astype(jnp.float32).reshape(TOKENS, TOP, D)
    outputs = jnp.sum(gates[:, :, None] * per_route, axis=1).astype(jnp.bfloat16)
    route_grads = grad_rows[:route_total].astype(jnp.float32).reshape(TOKENS, TOP, D)
    input_grads = jnp.sum(route_grads, axis=1).astype(jnp.bfloat16)
    return (outputs, input_grads, expert_grads)
```

```python
import jax
import jax.numpy as jnp
from jax import lax
from jax.sharding import PartitionSpec as P

X_COUNT = 4
Y_COUNT = 2
Z_COUNT = 16
XY_COUNT = X_COUNT * Y_COUNT
CAP = 3


def xy_perm(value, dx, dy):
    pairs = []
    for source in range(X_COUNT * Y_COUNT * Z_COUNT):
        z = source % Z_COUNT
        y = (source // Z_COUNT) % Y_COUNT
        x = source // (Z_COUNT * Y_COUNT)
        dest = (((x + dx) % X_COUNT) * Y_COUNT + (y + dy) % Y_COUNT) * Z_COUNT + z
        pairs.append((source, dest))
    return lax.ppermute(value, "ep", pairs)


OFFSETS = [(k // Y_COUNT, k % Y_COUNT) for k in range(XY_COUNT)]


def xy_send(rows, sign):
    chunk = rows.shape[0] // XY_COUNT
    parts = []
    for k, (dx, dy) in enumerate(OFFSETS):
        part = rows[k * chunk : (k + 1) * chunk]
        parts.append(part if k == 0 else xy_perm(part, sign * dx, sign * dy))
    return jnp.concatenate(parts, axis=0)


def z_exchange(rows):
    groups = [[xy * Z_COUNT + z for z in range(Z_COUNT)] for xy in range(XY_COUNT)]
    chunk = rows.shape[0] // Z_COUNT
    moved = lax.all_to_all(
        rows.reshape(Z_COUNT, chunk, rows.shape[1]),
        "ep",
        split_axis=0,
        concat_axis=0,
        tiled=True,
        axis_index_groups=groups,
    )
    return moved.reshape(rows.shape)


def pick(one_hot, rows, contract):
    return lax.dot_general(
        one_hot, rows, (((contract,), (0,)), ((), ())), preferred_element_type=jnp.float32
    )


def body(tokens, cotangent, experts, gates, weights, swap_flags):
    ep_count = lax.axis_size("ep")
    half_ep = ep_count // 2
    tok_rows, feature_dim = tokens.shape
    route_count = experts.shape[1]
    slot_count = ep_count * CAP
    my_index = lax.axis_index("ep")
    pair_lanes = jnp.arange(half_ep, dtype=jnp.int32)

    my_flag = jnp.sum(jnp.where(pair_lanes == my_index % half_ep, swap_flags, 0)) > 0
    own_weights = weights[0]
    swap_pairs = [(source, source ^ half_ep) for source in range(ep_count)]
    partner = lax.ppermute(own_weights, "ep", swap_pairs)
    own_weights = jnp.where(my_flag, partner, own_weights)
    full_weights = lax.all_gather(own_weights, "dp", axis=1, tiled=True)

    routed = experts.reshape(-1)
    flagged = (
        jnp.sum(
            jnp.where((routed % half_ep)[:, None] == pair_lanes[None, :], swap_flags[None, :], 0),
            axis=1,
        )
        > 0
    )
    target = jnp.where(flagged, (routed + half_ep) % ep_count, routed)
    order = jnp.arange(tok_rows * route_count, dtype=jnp.int32)
    same = (target[:, None] == target[None, :]) & (order[:, None] > order[None, :])
    rank = jnp.sum(same.astype(jnp.int32), axis=1)
    slot = (target % Z_COUNT) * (XY_COUNT * CAP) + (target // Z_COUNT) * CAP + rank
    slot = slot.reshape(tok_rows, route_count)
    lanes = jnp.arange(slot_count, dtype=jnp.int32)[:, None]
    hits = [lanes == slot[:, k][None, :] for k in range(route_count)]
    placers = [hit.astype(jnp.bfloat16) for hit in hits]
    token_placer = (hits[0] | hits[1]).astype(jnp.bfloat16)
    slot_gate = sum(
        jnp.sum(jnp.where(hits[k], gates[:, k][None, :], 0.0), axis=1) for k in range(route_count)
    )

    row_id = jnp.arange(slot_count, dtype=jnp.int32)
    my_xy = my_index // Z_COUNT
    k_of = row_id // (Z_COUNT * CAP)
    z_of = (row_id // CAP) % Z_COUNT
    r_of = row_id % CAP
    to_x = (my_xy // Y_COUNT + k_of // Y_COUNT) % X_COUNT
    to_y = (my_xy % Y_COUNT + k_of % Y_COUNT) % Y_COUNT
    from_row = z_of * (XY_COUNT * CAP) + (to_x * Y_COUNT + to_y) * CAP + r_of
    perm = (from_row[:, None] == row_id[None, :]).astype(jnp.bfloat16)

    send_x = pick(token_placer, tokens, 1).astype(jnp.bfloat16)
    z_x = z_exchange(send_x)
    send_dy = (slot_gate[:, None] * pick(token_placer, cotangent, 1)).astype(jnp.bfloat16)
    send_dy, z_x = lax.optimization_barrier((send_dy, z_x))
    z_dy = z_exchange(send_dy)

    rows_x = xy_send(pick(perm, z_x, 1).astype(jnp.bfloat16), 1)
    w_gate, w_up, w_down = (full_weights[0], full_weights[1], full_weights[2])
    pre_gate = jnp.dot(rows_x, w_gate, preferred_element_type=jnp.float32)
    pre_up = jnp.dot(rows_x, w_up, preferred_element_type=jnp.float32)
    gate_sig = jax.nn.sigmoid(pre_gate)
    gate_act = pre_gate * gate_sig
    hidden = (gate_act * pre_up).astype(jnp.bfloat16)
    expert_out = jnp.einsum("rf,df->rd", hidden, w_down, preferred_element_type=jnp.float32).astype(
        jnp.bfloat16
    )
    home_y = pick(perm, xy_send(expert_out, -1), 0).astype(jnp.bfloat16)
    home_y, z_dy = lax.optimization_barrier((home_y, z_dy))
    back_y = z_exchange(home_y)

    rows_dy = xy_send(pick(perm, z_dy, 1).astype(jnp.bfloat16), 1)
    hidden_grad = jnp.dot(rows_dy, w_down, preferred_element_type=jnp.float32)
    gate_pre = (hidden_grad * pre_up * gate_sig * (1.0 + pre_gate * (1.0 - gate_sig))).astype(
        jnp.bfloat16
    )
    up_pre = (hidden_grad * gate_act).astype(jnp.bfloat16)
    paired = jnp.concatenate([gate_pre, up_pre], axis=1)
    w_pair = jnp.concatenate([w_gate, w_up], axis=1)
    in_grad = jnp.einsum("rf,df->rd", paired, w_pair, preferred_element_type=jnp.float32).astype(
        jnp.bfloat16
    )
    home_dx = pick(perm, xy_send(in_grad, -1), 0).astype(jnp.bfloat16)
    home_dx, back_y = lax.optimization_barrier((home_dx, back_y))
    back_dx = z_exchange(home_dx)

    unit_count = hidden.shape[1]
    pair_term = jnp.einsum("rc,rf->cf", rows_x, paired, preferred_element_type=jnp.float32)
    down_term = jnp.einsum("rd,rf->df", rows_dy, hidden, preferred_element_type=jnp.float32)
    pair_grad = lax.psum_scatter(
        pair_term.astype(jnp.bfloat16), "dp", scatter_dimension=0, tiled=True
    )
    down_mine = lax.psum_scatter(
        down_term.astype(jnp.bfloat16), "dp", scatter_dimension=0, tiled=True
    )
    weight_grads = jnp.stack(
        [pair_grad[:, :unit_count], pair_grad[:, unit_count:], down_mine]
    )[None]

    outputs = sum(
        gates[:, k][:, None] * pick(placers[k], back_y, 0) for k in range(route_count)
    ).astype(jnp.bfloat16)
    input_grads = pick(token_placer, back_dx, 0).astype(jnp.bfloat16)
    return (outputs, input_grads, weight_grads)


def solution(mesh):
    return jax.shard_map(
        body,
        mesh=mesh,
        in_specs=(
            P(("ep", "dp"), None),
            P(("ep", "dp"), None),
            P(("ep", "dp"), None),
            P(("ep", "dp"), None),
            P("ep", None, "dp", None),
            P(),
        ),
        out_specs=(P(("ep", "dp"), None), P(("ep", "dp"), None), P("ep", None, "dp", None)),
        check_vma=False,
    )
```

```python
import jax
import jax.numpy as jnp
import numpy as np
from jax import lax
from jax.experimental import pallas as pl
from jax.experimental.pallas import tpu as pltpu
from jax.sharding import PartitionSpec as P

CAP = 3
QUARTERS = 4
GROUP = 16
CHUNK = 2 * QUARTERS * CAP
BLOCK = GROUP * CHUNK
LANES = GROUP * CAP
MIB = 1 << 20


def unfold_matrix():
    row = np.arange(BLOCK)
    array, quarter = row // (BLOCK // 2), (row // LANES) % QUARTERS
    peer, route = (row % LANES) // CAP, row % CAP
    source = peer * CHUNK + array * (CHUNK // 2) + quarter * CAP + route
    return (source[:, None] == row[None, :]).astype(np.float32)


def fold_block(block, first, second, fold):
    width = first.shape[1] // QUARTERS
    rows = slice(block * LANES, (block + 1) * LANES)
    parts = [
        ref[rows, q * width : (q + 1) * width] for ref in (first, second) for q in range(QUARTERS)
    ]
    stacked = jnp.concatenate(parts, axis=0)
    return jnp.dot(fold, stacked, preferred_element_type=jnp.float32).astype(jnp.bfloat16)


def unfold_block(block, chunks, unfold, first, second):
    width = chunks.shape[1]
    rows = slice(block * LANES, (block + 1) * LANES)
    opened = jnp.dot(unfold, chunks, preferred_element_type=jnp.float32).astype(jnp.bfloat16)
    for index, ref in enumerate((first, second)):
        for q in range(QUARTERS):
            start = (index * QUARTERS + q) * LANES
            ref[rows, q * width : (q + 1) * width] = opened[start : start + LANES]


def prep_kernel(
    tok_ref, cot_ref, ecol_ref, erow_ref, grow_ref, fcol_ref, frow_ref, fold_ref,
    send_ref, scol_ref, srow_ref, x_ref, dy_ref, out_ref, sems,
):
    tok_rows, feature_dim = tok_ref.shape
    half = frow_ref.shape[1]
    slot_count = x_ref.shape[0]

    def flag_bit(mask, flags, axis):
        return jnp.sum(jnp.where(mask, flags, 0), axis=axis, keepdims=True) * half

    tcol, trow = [], []
    for k in range(2):
        col, row = ecol_ref[:, k : k + 1], erow_ref[k : k + 1, :]
        lane = lax.broadcasted_iota(jnp.int32, (tok_rows, half), 1)
        sub = lax.broadcasted_iota(jnp.int32, (half, tok_rows), 0)
        tcol.append(col ^ flag_bit((col & (half - 1)) == lane, frow_ref[...], 1))
        trow.append(row ^ flag_bit((row & (half - 1)) == sub, fcol_ref[...], 0))
    sub = lax.broadcasted_iota(jnp.int32, (tok_rows, tok_rows), 0)
    lane = lax.broadcasted_iota(jnp.int32, (tok_rows, tok_rows), 1)
    srows = []
    for k in range(2):
        rank_row = jnp.zeros((1, tok_rows), jnp.int32)
        rank_col = jnp.zeros((tok_rows, 1), jnp.int32)
        for j in range(2):
            above = sub * 2 + j < lane * 2 + k
            hit = (tcol[j] == trow[k]) & above
            rank_row += jnp.sum(jnp.where(hit, 1, 0), axis=0, keepdims=True)
            before = lane * 2 + j < sub * 2 + k
            hit = (tcol[k] == trow[j]) & before
            rank_col += jnp.sum(jnp.where(hit, 1, 0), axis=1, keepdims=True)
        srows.append(trow[k] * CAP + rank_row)
        srow_ref[k : k + 1, :] = srows[k]
        scol_ref[:, k : k + 1] = tcol[k] * CAP + rank_col
    slot = lax.broadcasted_iota(jnp.int32, (slot_count, tok_rows), 0)
    hits = [slot == srows[k] for k in range(2)]
    gate = sum(
        jnp.sum(jnp.where(hits[k], grow_ref[k : k + 1, :], 0.0), axis=1, keepdims=True)
        for k in range(2)
    )
    placer = jnp.where(hits[0] | hits[1], 1.0, 0.0).astype(jnp.bfloat16)
    width = feature_dim // QUARTERS
    for q in range(QUARTERS):
        cols = slice(q * width, (q + 1) * width)
        x = jnp.dot(placer, tok_ref[:, cols], preferred_element_type=jnp.float32)
        x_ref[:, cols] = x.astype(jnp.bfloat16)
        dy = jnp.dot(placer, cot_ref[:, cols], preferred_element_type=jnp.float32)
        dy_ref[:, cols] = (gate * dy).astype(jnp.bfloat16)
    fold = fold_ref[...]
    copies = []
    for b in range(slot_count // LANES):
        out_ref[b] = fold_block(b, x_ref, dy_ref, fold)
        copies.append(pltpu.make_async_copy(out_ref.at[b], send_ref.at[b], sems.at[b]))
        copies[b].start()
    for copy in copies:
        copy.wait()


def expert_kernel(
    recv_ref, w_ref, unfold_ref, fold_ref,
    send_ref, x_out, dy_out, hidden_ref, paired_ref,
    chunk_ref, wv_ref, x_ref, dy_ref, y_ref, dx_ref, r_sems, w_sems, s_sems, u_sems,
):
    blocks = chunk_ref.shape[0]
    feature_dim = x_ref.shape[1]
    units = hidden_ref.shape[1]
    arrivals = [
        pltpu.make_async_copy(recv_ref.at[b], chunk_ref.at[b], r_sems.at[b]) for b in range(blocks)
    ]
    loads = [pltpu.make_async_copy(w_ref.at[i], wv_ref.at[i], w_sems.at[i]) for i in range(3)]
    for copy in arrivals + loads:
        copy.start()
    unfold = unfold_ref[...]
    for b in range(blocks):
        arrivals[b].wait()
        unfold_block(b, chunk_ref[b], unfold, x_ref, dy_ref)
    keeps = [
        pltpu.make_async_copy(x_ref, x_out, u_sems.at[0]),
        pltpu.make_async_copy(dy_ref, dy_out, u_sems.at[1]),
    ]
    for copy in keeps:
        copy.start()
    for copy in loads:
        copy.wait()
    x, dy = x_ref[...], dy_ref[...]
    pre_gate = jnp.dot(x, wv_ref[0], preferred_element_type=jnp.float32)
    pre_up = jnp.dot(x, wv_ref[1], preferred_element_type=jnp.float32)
    hidden_grad = jnp.dot(dy, wv_ref[2], preferred_element_type=jnp.float32)
    gate_sig = jax.nn.sigmoid(pre_gate)
    gate_act = pre_gate * gate_sig
    hidden = (gate_act * pre_up).astype(jnp.bfloat16)
    gate_pre = (hidden_grad * pre_up * gate_sig * (1.0 + pre_gate * (1.0 - gate_sig))).astype(
        jnp.bfloat16
    )
    up_pre = (hidden_grad * gate_act).astype(jnp.bfloat16)
    hidden_ref[...] = hidden
    paired_ref[:, :units] = gate_pre
    paired_ref[:, units:] = up_pre
    across = (((1,), (1,)), ((), ()))
    width = feature_dim // QUARTERS
    for q in range(QUARTERS):
        cols = slice(q * width, (q + 1) * width)
        y = lax.dot_general(hidden, wv_ref[2, cols, :], across, preferred_element_type=jnp.float32)
        y_ref[:, cols] = y.astype(jnp.bfloat16)
        dx = lax.dot_general(
            gate_pre, wv_ref[0, cols, :], across, preferred_element_type=jnp.float32
        ) + lax.dot_general(up_pre, wv_ref[1, cols, :], across, preferred_element_type=jnp.float32)
        dx_ref[:, cols] = dx.astype(jnp.bfloat16)
    fold = fold_ref[...]
    copies = []
    for b in range(blocks):
        chunk_ref[b] = fold_block(b, y_ref, dx_ref, fold)
        copies.append(pltpu.make_async_copy(chunk_ref.at[b], send_ref.at[b], s_sems.at[b]))
        copies[b].start()
    for copy in keeps + copies:
        copy.wait()


def finish_kernel(
    recv_ref, scol_ref, gates_ref, unfold_ref, out_ref, grad_ref, chunk_ref, y_ref, dx_ref, sems,
):
    blocks = chunk_ref.shape[0]
    tok_rows, feature_dim = out_ref.shape
    slot_count = y_ref.shape[0]
    arrivals = [
        pltpu.make_async_copy(recv_ref.at[b], chunk_ref.at[b], sems.at[b]) for b in range(blocks)
    ]
    for copy in arrivals:
        copy.start()
    slot = lax.broadcasted_iota(jnp.int32, (tok_rows, slot_count), 1)
    hits = [slot == scol_ref[:, k : k + 1] for k in range(2)]
    takers = [jnp.where(hit, 1.0, 0.0).astype(jnp.bfloat16) for hit in hits]
    both = jnp.where(hits[0] | hits[1], 1.0, 0.0).astype(jnp.bfloat16)
    unfold = unfold_ref[...]
    for b in range(blocks):
        arrivals[b].wait()
        unfold_block(b, chunk_ref[b], unfold, y_ref, dx_ref)
    width = feature_dim // QUARTERS
    for q in range(QUARTERS):
        cols = slice(q * width, (q + 1) * width)
        total = sum(
            gates_ref[:, k : k + 1]
            * jnp.dot(takers[k], y_ref[:, cols], preferred_element_type=jnp.float32)
            for k in range(2)
        )
        out_ref[:, cols] = total.astype(jnp.bfloat16)
        grad = jnp.dot(both, dx_ref[:, cols], preferred_element_type=jnp.float32)
        grad_ref[:, cols] = grad.astype(jnp.bfloat16)


def exchange(chunks, ep_count):
    width = chunks.shape[-1]
    moved = lax.all_to_all(
        chunks.reshape(ep_count, CHUNK, width), "ep", split_axis=0, concat_axis=0, tiled=True
    )
    return moved.reshape(chunks.shape)


def body(tokens, cotangent, experts, gates, weights, swap_flags):
    ep_count = lax.axis_size("ep")
    half_ep = ep_count // 2
    tok_rows, feature_dim = tokens.shape
    slot_count = ep_count * CAP
    blocks = ep_count // GROUP
    units = weights.shape[3]
    width = feature_dim // QUARTERS
    my_index = lax.axis_index("ep")
    bf16 = jnp.bfloat16
    vmem, hbm = pl.BlockSpec(memory_space=pltpu.VMEM), pl.BlockSpec(memory_space=pl.ANY)
    unfold = unfold_matrix()
    fold = jnp.asarray(unfold.T, bf16)
    unfold = jnp.asarray(unfold, bf16)
    chunks_shape = jax.ShapeDtypeStruct((blocks, BLOCK, width), bf16)
    rows_shape = jax.ShapeDtypeStruct((slot_count, feature_dim), bf16)
    rows_vmem = pltpu.VMEM((slot_count, feature_dim), bf16)
    chunks_vmem = pltpu.VMEM((blocks, BLOCK, width), bf16)
    block_sems = pltpu.SemaphoreType.DMA((blocks,))

    send, slot_col, _ = pl.pallas_call(
        prep_kernel,
        out_shape=(
            chunks_shape,
            jax.ShapeDtypeStruct((tok_rows, 2), jnp.int32),
            jax.ShapeDtypeStruct((2, tok_rows), jnp.int32),
        ),
        in_specs=[vmem] * 8,
        out_specs=(hbm, vmem, vmem),
        scratch_shapes=[rows_vmem, rows_vmem, chunks_vmem, block_sems],
        compiler_params=pltpu.CompilerParams(vmem_limit_bytes=24 * MIB),
        name="prep",
    )(
        tokens, cotangent, experts, experts.T, gates.T,
        swap_flags.reshape(half_ep, 1), swap_flags.reshape(1, half_ep), fold,
    )

    pair_lanes = jnp.arange(half_ep, dtype=jnp.int32)
    my_flag = jnp.sum(jnp.where(pair_lanes == my_index % half_ep, swap_flags, 0)) > 0
    own_weights = weights[0]
    swap_pairs = [(source, source ^ half_ep) for source in range(ep_count)]
    partner = lax.ppermute(own_weights, "ep", swap_pairs)
    own_weights = jnp.where(my_flag, partner, own_weights)
    full_weights = lax.all_gather(own_weights, "dp", axis=1, tiled=True)

    recv = exchange(send, ep_count)

    send_back, rows_x, rows_dy, hidden, paired = pl.pallas_call(
        expert_kernel,
        out_shape=(
            chunks_shape,
            rows_shape,
            rows_shape,
            jax.ShapeDtypeStruct((slot_count, units), bf16),
            jax.ShapeDtypeStruct((slot_count, 2 * units), bf16),
        ),
        in_specs=[hbm, hbm, vmem, vmem],
        out_specs=(hbm, hbm, hbm, vmem, vmem),
        scratch_shapes=[
            chunks_vmem,
            pltpu.VMEM((3, feature_dim, units), bf16),
            rows_vmem,
            rows_vmem,
            rows_vmem,
            rows_vmem,
            block_sems,
            pltpu.SemaphoreType.DMA((3,)),
            block_sems,
            pltpu.SemaphoreType.DMA((2,)),
        ],
        compiler_params=pltpu.CompilerParams(vmem_limit_bytes=44 * MIB),
        name="expert",
    )(recv, full_weights, unfold, fold)

    recv_back = exchange(send_back, ep_count)

    pair_term = jnp.einsum("rc,rf->cf", rows_x, paired, preferred_element_type=jnp.float32)
    down_term = jnp.einsum("rd,rf->df", rows_dy, hidden, preferred_element_type=jnp.float32)
    terms = jnp.concatenate([pair_term.astype(bf16), down_term.astype(bf16)], axis=1)
    mine = lax.psum_scatter(terms, "dp", scatter_dimension=0, tiled=True)
    weight_grads = jnp.stack(
        [mine[:, :units], mine[:, units : 2 * units], mine[:, 2 * units :]]
    )[None]

    outputs, input_grads = pl.pallas_call(
        finish_kernel,
        out_shape=(
            jax.ShapeDtypeStruct((tok_rows, feature_dim), bf16),
            jax.ShapeDtypeStruct((tok_rows, feature_dim), bf16),
        ),
        in_specs=[hbm, vmem, vmem, vmem],
        out_specs=(vmem, vmem),
        scratch_shapes=[chunks_vmem, rows_vmem, rows_vmem, block_sems],
        compiler_params=pltpu.CompilerParams(vmem_limit_bytes=24 * MIB),
        name="finish",
    )(recv_back, slot_col, gates, unfold)
    return (outputs, input_grads, weight_grads)


def solution(mesh):
    return jax.shard_map(
        body,
        mesh=mesh,
        in_specs=(
            P(("ep", "dp"), None),
            P(("ep", "dp"), None),
            P(("ep", "dp"), None),
            P(("ep", "dp"), None),
            P("ep", None, "dp", None),
            P(),
        ),
        out_specs=(P(("ep", "dp"), None), P(("ep", "dp"), None), P("ep", None, "dp", None)),
        check_vma=False,
    )
```

```python
import jax
import jax.numpy as jnp
import numpy as np
from jax import lax
from jax.experimental import pallas as pl
from jax.experimental.pallas import tpu as pltpu
from jax.sharding import PartitionSpec as P

CAP = 3
QUARTERS = 4
GROUP = 16
CHUNK = 2 * QUARTERS * CAP
BLOCK = GROUP * CHUNK
LANES = GROUP * CAP
MIB = 1 << 20
VMEM_MIB = 60
EXPERT_MIB = 53


def unfold_matrix():
    row = np.arange(BLOCK)
    array, quarter = row // (BLOCK // 2), (row // LANES) % QUARTERS
    peer, route = (row % LANES) // CAP, row % CAP
    source = peer * CHUNK + array * (CHUNK // 2) + quarter * CAP + route
    return (source[:, None] == row[None, :]).astype(np.float32)


def fold_block(block, first, second, fold):
    width = first.shape[1] // QUARTERS
    rows = slice(block * LANES, (block + 1) * LANES)
    parts = [
        ref[rows, q * width : (q + 1) * width] for ref in (first, second) for q in range(QUARTERS)
    ]
    stacked = jnp.concatenate(parts, axis=0)
    return jnp.dot(fold, stacked, preferred_element_type=jnp.float32).astype(jnp.bfloat16)


def unfold_block(block, chunks, unfold, first, second):
    width = chunks.shape[1]
    rows = slice(block * LANES, (block + 1) * LANES)
    opened = jnp.dot(unfold, chunks, preferred_element_type=jnp.float32).astype(jnp.bfloat16)
    for index, ref in enumerate((first, second)):
        for q in range(QUARTERS):
            start = (index * QUARTERS + q) * LANES
            ref[rows, q * width : (q + 1) * width] = opened[start : start + LANES]


def column(row):
    n = row.shape[1]
    same = lax.broadcasted_iota(jnp.int32, (n, n), 0) == lax.broadcasted_iota(jnp.int32, (n, n), 1)
    return jnp.sum(jnp.where(same, row, jnp.zeros_like(row)), axis=1, keepdims=True)


def start_all(copies):
    for copy in copies:
        copy.start()
    return copies


def prep_kernel(
    tok_hbm, cot_hbm, experts_hbm, gates_hbm, flags_hbm, fold_hbm,
    send_hbm, slots_hbm,
    tok_ref, cot_ref, experts_ref, gates_ref, flags_ref, fold_ref, slots_ref, x_ref, dy_ref, out_ref,
    in_sems, out_sems, slot_sem,
):
    tok_rows, feature_dim = tok_ref.shape
    half = flags_ref.shape[1]
    slot_count = x_ref.shape[0]
    pairs = [
        (experts_hbm, experts_ref), (flags_hbm, flags_ref), (gates_hbm, gates_ref),
        (tok_hbm, tok_ref), (cot_hbm, cot_ref), (fold_hbm, fold_ref),
    ]
    loads = start_all(
        [pltpu.make_async_copy(src, dst, in_sems.at[i]) for i, (src, dst) in enumerate(pairs)]
    )
    loads[0].wait()
    loads[1].wait()
    flags = column(flags_ref[...])
    trow = []
    for k in range(2):
        row = experts_ref[k : k + 1, :]
        sub = lax.broadcasted_iota(jnp.int32, (half, tok_rows), 0)
        mine = jnp.sum(jnp.where((row & (half - 1)) == sub, flags, 0), axis=0, keepdims=True)
        trow.append(row ^ (mine * half))
    tcol = [column(row) for row in trow]
    sub = lax.broadcasted_iota(jnp.int32, (tok_rows, tok_rows), 0)
    lane = lax.broadcasted_iota(jnp.int32, (tok_rows, tok_rows), 1)
    slots = []
    for k in range(2):
        rank = jnp.zeros((1, tok_rows), jnp.int32)
        for j in range(2):
            hit = (tcol[j] == trow[k]) & (sub * 2 + j < lane * 2 + k)
            rank += jnp.sum(jnp.where(hit, 1, 0), axis=0, keepdims=True)
        slots.append(trow[k] * CAP + rank)
        slots_ref[k : k + 1, :] = slots[k]
    keep = pltpu.make_async_copy(slots_ref, slots_hbm, slot_sem)
    keep.start()
    slot = lax.broadcasted_iota(jnp.int32, (slot_count, tok_rows), 0)
    hits = [slot == slots[k] for k in range(2)]
    loads[2].wait()
    gate = sum(
        jnp.sum(jnp.where(hits[k], gates_ref[k : k + 1, :], 0.0), axis=1, keepdims=True)
        for k in range(2)
    )
    placer = jnp.where(hits[0] | hits[1], 1.0, 0.0).astype(jnp.bfloat16)
    for copy in loads[3:]:
        copy.wait()
    width = feature_dim // QUARTERS
    for q in range(QUARTERS):
        cols = slice(q * width, (q + 1) * width)
        x = jnp.dot(placer, tok_ref[:, cols], preferred_element_type=jnp.float32)
        x_ref[:, cols] = x.astype(jnp.bfloat16)
        dy = jnp.dot(placer, cot_ref[:, cols], preferred_element_type=jnp.float32)
        dy_ref[:, cols] = (gate * dy).astype(jnp.bfloat16)
    fold = fold_ref[...]
    copies = [keep]
    for b in range(slot_count // LANES):
        out_ref[b] = fold_block(b, x_ref, dy_ref, fold)
        copies += start_all(
            [pltpu.make_async_copy(out_ref.at[b], send_hbm.at[b], out_sems.at[b])]
        )
    for copy in copies:
        copy.wait()


def expert_kernel(
    recv_hbm, ahead_hbm, back_hbm, unfold_hbm, fold_hbm,
    send_hbm, x_hbm, dy_hbm, hidden_hbm, paired_hbm,
    chunk_ref, ahead_ref, back_ref, unfold_ref, fold_ref,
    x_ref, dy_ref, hidden_ref, paired_ref, y_ref, dx_ref,
    recv_sems, load_sems, send_sems, keep_sems,
):
    blocks = chunk_ref.shape[0]
    feature_dim = x_ref.shape[1]
    units = hidden_ref.shape[1]
    pairs = [(unfold_hbm, unfold_ref), (fold_hbm, fold_ref)]
    pairs += [(ahead_hbm.at[i], ahead_ref.at[i]) for i in range(3)] + [(back_hbm, back_ref)]
    loads = [
        pltpu.make_async_copy(src, dst, load_sems.at[i]) for i, (src, dst) in enumerate(pairs)
    ]
    loads[0].start()
    arrivals = start_all(
        [
            pltpu.make_async_copy(recv_hbm.at[b], chunk_ref.at[b], recv_sems.at[b])
            for b in range(blocks)
        ]
    )
    start_all(loads[1:])
    loads[0].wait()
    unfold = unfold_ref[...]
    for b in range(blocks):
        arrivals[b].wait()
        unfold_block(b, chunk_ref[b], unfold, x_ref, dy_ref)
    copies = start_all(
        [
            pltpu.make_async_copy(x_ref, x_hbm, keep_sems.at[0]),
            pltpu.make_async_copy(dy_ref, dy_hbm, keep_sems.at[1]),
        ]
    )
    for copy in loads[1:]:
        copy.wait()
    pre_gate = jnp.dot(x_ref[...], ahead_ref[0], preferred_element_type=jnp.float32)
    pre_up = jnp.dot(x_ref[...], ahead_ref[1], preferred_element_type=jnp.float32)
    hidden_grad = jnp.dot(dy_ref[...], ahead_ref[2], preferred_element_type=jnp.float32)
    gate_sig = jax.nn.sigmoid(pre_gate)
    gate_act = pre_gate * gate_sig
    hidden_ref[...] = (gate_act * pre_up).astype(jnp.bfloat16)
    gate_pre = hidden_grad * pre_up * gate_sig * (1.0 + pre_gate * (1.0 - gate_sig))
    paired_ref[:, :units] = gate_pre.astype(jnp.bfloat16)
    paired_ref[:, units:] = (hidden_grad * gate_act).astype(jnp.bfloat16)
    copies += start_all(
        [
            pltpu.make_async_copy(hidden_ref, hidden_hbm, keep_sems.at[2]),
            pltpu.make_async_copy(paired_ref, paired_hbm, keep_sems.at[3]),
        ]
    )
    width = feature_dim // QUARTERS
    for q in range(QUARTERS):
        cols = slice(q * width, (q + 1) * width)
        y = jnp.dot(
            hidden_ref[...], back_ref[2 * units :, cols], preferred_element_type=jnp.float32
        )
        y_ref[:, cols] = y.astype(jnp.bfloat16)
        dx = jnp.dot(
            paired_ref[...], back_ref[: 2 * units, cols], preferred_element_type=jnp.float32
        )
        dx_ref[:, cols] = dx.astype(jnp.bfloat16)
    fold = fold_ref[...]
    for b in range(blocks):
        chunk_ref[b] = fold_block(b, y_ref, dx_ref, fold)
        copies += start_all(
            [pltpu.make_async_copy(chunk_ref.at[b], send_hbm.at[b], send_sems.at[b])]
        )
    for copy in copies:
        copy.wait()


def finish_kernel(
    recv_hbm, slots_hbm, gates_hbm, unfold_hbm,
    outputs_hbm, grads_hbm,
    chunk_ref, slots_ref, gates_ref, unfold_ref,
    y_ref, dx_ref, outputs_ref, grads_ref, recv_sems, load_sems, sems,
):
    blocks = chunk_ref.shape[0]
    pairs = [(slots_hbm, slots_ref), (gates_hbm, gates_ref), (unfold_hbm, unfold_ref)]
    loads = start_all(
        [pltpu.make_async_copy(src, dst, load_sems.at[i]) for i, (src, dst) in enumerate(pairs)]
    )
    arrivals = start_all(
        [
            pltpu.make_async_copy(recv_hbm.at[b], chunk_ref.at[b], recv_sems.at[b])
            for b in range(blocks)
        ]
    )
    for copy in loads:
        copy.wait()
    tok_rows, feature_dim = outputs_ref.shape
    slot_count = y_ref.shape[0]
    slot = lax.broadcasted_iota(jnp.int32, (tok_rows, slot_count), 1)
    hits = [slot == column(slots_ref[k : k + 1, :]) for k in range(2)]
    gates = [column(gates_ref[k : k + 1, :]) for k in range(2)]
    takers = [jnp.where(hit, 1.0, 0.0).astype(jnp.bfloat16) for hit in hits]
    both = jnp.where(hits[0] | hits[1], 1.0, 0.0).astype(jnp.bfloat16)
    unfold = unfold_ref[...]
    for b in range(blocks):
        arrivals[b].wait()
        unfold_block(b, chunk_ref[b], unfold, y_ref, dx_ref)
    width = feature_dim // QUARTERS
    copies = []
    for q in range(QUARTERS):
        cols = slice(q * width, (q + 1) * width)
        total = sum(
            gates[k] * jnp.dot(takers[k], y_ref[:, cols], preferred_element_type=jnp.float32)
            for k in range(2)
        )
        outputs_ref[:, cols] = total.astype(jnp.bfloat16)
        grad = jnp.dot(both, dx_ref[:, cols], preferred_element_type=jnp.float32)
        grads_ref[:, cols] = grad.astype(jnp.bfloat16)
        copies += start_all(
            [
                pltpu.make_async_copy(
                    outputs_ref.at[:, cols], outputs_hbm.at[:, cols], sems.at[2 * q]
                ),
                pltpu.make_async_copy(
                    grads_ref.at[:, cols], grads_hbm.at[:, cols], sems.at[2 * q + 1]
                ),
            ]
        )
    for copy in copies:
        copy.wait()


def exchange(chunks, ep_count):
    width = chunks.shape[-1]
    moved = lax.all_to_all(
        chunks.reshape(ep_count, CHUNK, width), "ep", split_axis=0, concat_axis=0, tiled=True
    )
    return moved.reshape(chunks.shape)


def body(tokens, cotangent, experts, gates, weights, swap_flags):
    ep_count = lax.axis_size("ep")
    half_ep = ep_count // 2
    tok_rows, feature_dim = tokens.shape
    slot_count = ep_count * CAP
    blocks = ep_count // GROUP
    units = weights.shape[3]
    width = feature_dim // QUARTERS
    my_index = lax.axis_index("ep")
    bf16 = jnp.bfloat16
    hbm = pl.BlockSpec(memory_space=pltpu.HBM)
    dma = pltpu.SemaphoreType.DMA
    unfold = unfold_matrix()
    fold = jnp.asarray(unfold.T, bf16)
    unfold = jnp.asarray(unfold, bf16)
    chunks_shape = jax.ShapeDtypeStruct((blocks, BLOCK, width), bf16)
    rows_shape = jax.ShapeDtypeStruct((slot_count, feature_dim), bf16)
    tok_shape = jax.ShapeDtypeStruct((tok_rows, feature_dim), bf16)
    hidden_shape = jax.ShapeDtypeStruct((slot_count, units), bf16)
    paired_shape = jax.ShapeDtypeStruct((slot_count, 2 * units), bf16)
    slots_shape = jax.ShapeDtypeStruct((2, tok_rows), jnp.int32)

    def scratch(shape):
        return pltpu.VMEM(shape.shape, shape.dtype)

    gate_rows = gates.T
    send, slots = pl.pallas_call(
        prep_kernel,
        out_shape=(chunks_shape, slots_shape),
        in_specs=[hbm] * 6,
        out_specs=(hbm, hbm),
        scratch_shapes=[
            scratch(tok_shape),
            scratch(tok_shape),
            scratch(slots_shape),
            pltpu.VMEM((2, tok_rows), jnp.float32),
            pltpu.VMEM((1, half_ep), jnp.int32),
            pltpu.VMEM((BLOCK, BLOCK), bf16),
            scratch(slots_shape),
            scratch(rows_shape),
            scratch(rows_shape),
            scratch(chunks_shape),
            dma((6,)),
            dma((blocks,)),
            dma,
        ],
        compiler_params=pltpu.CompilerParams(vmem_limit_bytes=VMEM_MIB * MIB),
        name="prep",
    )(tokens, cotangent, experts.T, gate_rows, swap_flags.reshape(1, half_ep), fold)

    pair_lanes = jnp.arange(half_ep, dtype=jnp.int32)
    my_flag = jnp.sum(jnp.where(pair_lanes == my_index % half_ep, swap_flags, 0)) > 0
    own_weights = weights[0]
    swap_pairs = [(source, source ^ half_ep) for source in range(ep_count)]
    partner = lax.ppermute(own_weights, "ep", swap_pairs)
    own_weights = jnp.where(my_flag, partner, own_weights)
    full_weights = lax.all_gather(own_weights, "dp", axis=1, tiled=True)
    back = full_weights.transpose(0, 2, 1).reshape(3 * units, feature_dim)

    recv = exchange(send, ep_count)

    send_back, rows_x, rows_dy, hidden, paired = pl.pallas_call(
        expert_kernel,
        out_shape=(chunks_shape, rows_shape, rows_shape, hidden_shape, paired_shape),
        in_specs=[hbm] * 5,
        out_specs=(hbm,) * 5,
        scratch_shapes=[
            scratch(chunks_shape),
            pltpu.VMEM((3, feature_dim, units), bf16),
            pltpu.VMEM((3 * units, feature_dim), bf16),
            pltpu.VMEM((BLOCK, BLOCK), bf16),
            pltpu.VMEM((BLOCK, BLOCK), bf16),
            scratch(rows_shape),
            scratch(rows_shape),
            scratch(hidden_shape),
            scratch(paired_shape),
            scratch(rows_shape),
            scratch(rows_shape),
            dma((blocks,)),
            dma((6,)),
            dma((blocks,)),
            dma((4,)),
        ],
        compiler_params=pltpu.CompilerParams(vmem_limit_bytes=EXPERT_MIB * MIB),
        name="expert",
    )(recv, full_weights, back, unfold, fold)

    recv_back = exchange(send_back, ep_count)

    pair_term = jnp.einsum("rc,rf->cf", rows_x, paired, preferred_element_type=jnp.float32)
    down_term = jnp.einsum("rd,rf->df", rows_dy, hidden, preferred_element_type=jnp.float32)
    terms = jnp.concatenate([pair_term.astype(bf16), down_term.astype(bf16)], axis=1)
    mine = lax.psum_scatter(terms, "dp", scatter_dimension=0, tiled=True)
    weight_grads = jnp.stack(
        [mine[:, :units], mine[:, units : 2 * units], mine[:, 2 * units :]]
    )[None]

    outputs, input_grads = pl.pallas_call(
        finish_kernel,
        out_shape=(tok_shape, tok_shape),
        in_specs=[hbm] * 4,
        out_specs=(hbm, hbm),
        scratch_shapes=[
            scratch(chunks_shape),
            scratch(slots_shape),
            pltpu.VMEM((2, tok_rows), jnp.float32),
            pltpu.VMEM((BLOCK, BLOCK), bf16),
            scratch(rows_shape),
            scratch(rows_shape),
            scratch(tok_shape),
            scratch(tok_shape),
            dma((blocks,)),
            dma((3,)),
            dma((2 * QUARTERS,)),
        ],
        compiler_params=pltpu.CompilerParams(vmem_limit_bytes=40 * MIB),
        name="finish",
    )(recv_back, slots, gate_rows, unfold)
    return (outputs, input_grads, weight_grads)


def solution(mesh):
    return jax.shard_map(
        body,
        mesh=mesh,
        in_specs=(
            P(("ep", "dp"), None),
            P(("ep", "dp"), None),
            P(("ep", "dp"), None),
            P(("ep", "dp"), None),
            P("ep", None, "dp", None),
            P(),
        ),
        out_specs=(P(("ep", "dp"), None), P(("ep", "dp"), None), P("ep", None, "dp", None)),
        check_vma=False,
    )
```

```python
import jax
import jax.numpy as jnp
import numpy as np
from jax import lax
from jax.experimental import pallas as pl
from jax.experimental.pallas import tpu as pltpu
from jax.sharding import PartitionSpec as P

CAP = 3
QUARTERS = 4
GROUP = 16
CHUNK = 2 * QUARTERS * CAP
BLOCK = GROUP * CHUNK
LANES = GROUP * CAP
MIB = 1 << 20
VMEM_MIB = 60
EXPERT_MIB = 53


def unfold_matrix():
    row = np.arange(BLOCK)
    array, quarter = row // (BLOCK // 2), (row // LANES) % QUARTERS
    peer, route = (row % LANES) // CAP, row % CAP
    source = peer * CHUNK + array * (CHUNK // 2) + quarter * CAP + route
    return (source[:, None] == row[None, :]).astype(np.float32)


def fold_block(block, first, second, fold):
    width = first.shape[1] // QUARTERS
    rows = slice(block * LANES, (block + 1) * LANES)
    parts = [
        ref[rows, q * width : (q + 1) * width] for ref in (first, second) for q in range(QUARTERS)
    ]
    stacked = jnp.concatenate(parts, axis=0)
    return jnp.dot(fold, stacked, preferred_element_type=jnp.float32).astype(jnp.bfloat16)


def unfold_block(block, chunks, unfold, first, second):
    width = chunks.shape[1]
    rows = slice(block * LANES, (block + 1) * LANES)
    opened = jnp.dot(unfold, chunks, preferred_element_type=jnp.float32).astype(jnp.bfloat16)
    for index, ref in enumerate((first, second)):
        for q in range(QUARTERS):
            start = (index * QUARTERS + q) * LANES
            ref[rows, q * width : (q + 1) * width] = opened[start : start + LANES]


def column(row):
    n = row.shape[1]
    same = lax.broadcasted_iota(jnp.int32, (n, n), 0) == lax.broadcasted_iota(jnp.int32, (n, n), 1)
    return jnp.sum(jnp.where(same, row, jnp.zeros_like(row)), axis=1, keepdims=True)


def start_all(copies):
    for copy in copies:
        copy.start()
    return copies


def prep_kernel(
    tok_hbm, cot_hbm, experts_hbm, gates_hbm, flags_hbm, fold_hbm,
    send_hbm, slots_hbm,
    tok_ref, cot_ref, experts_ref, gates_ref, flags_ref, fold_ref, slots_ref, x_ref, dy_ref, out_ref,
    in_sems, out_sems, slot_sem,
):
    tok_rows, feature_dim = tok_ref.shape
    half = flags_ref.shape[1]
    slot_count = x_ref.shape[0]
    pairs = [
        (experts_hbm, experts_ref), (flags_hbm, flags_ref), (gates_hbm, gates_ref),
        (tok_hbm, tok_ref), (cot_hbm, cot_ref), (fold_hbm, fold_ref),
    ]
    loads = start_all(
        [pltpu.make_async_copy(src, dst, in_sems.at[i]) for i, (src, dst) in enumerate(pairs)]
    )
    loads[0].wait()
    loads[1].wait()
    flags = column(flags_ref[...])
    trow = []
    for k in range(2):
        row = experts_ref[k : k + 1, :]
        sub = lax.broadcasted_iota(jnp.int32, (half, tok_rows), 0)
        mine = jnp.sum(jnp.where((row & (half - 1)) == sub, flags, 0), axis=0, keepdims=True)
        trow.append(row ^ (mine * half))
    tcol = [column(row) for row in trow]
    sub = lax.broadcasted_iota(jnp.int32, (tok_rows, tok_rows), 0)
    lane = lax.broadcasted_iota(jnp.int32, (tok_rows, tok_rows), 1)
    slots = []
    for k in range(2):
        rank = jnp.zeros((1, tok_rows), jnp.int32)
        for j in range(2):
            hit = (tcol[j] == trow[k]) & (sub * 2 + j < lane * 2 + k)
            rank += jnp.sum(jnp.where(hit, 1, 0), axis=0, keepdims=True)
        slots.append(trow[k] * CAP + rank)
        slots_ref[k : k + 1, :] = slots[k]
    keep = pltpu.make_async_copy(slots_ref, slots_hbm, slot_sem)
    keep.start()
    slot = lax.broadcasted_iota(jnp.int32, (slot_count, tok_rows), 0)
    hits = [slot == slots[k] for k in range(2)]
    loads[2].wait()
    gate = sum(
        jnp.sum(jnp.where(hits[k], gates_ref[k : k + 1, :], 0.0), axis=1, keepdims=True)
        for k in range(2)
    )
    placer = jnp.where(hits[0] | hits[1], 1.0, 0.0).astype(jnp.bfloat16)
    for copy in loads[3:]:
        copy.wait()
    width = feature_dim // QUARTERS
    for q in range(QUARTERS):
        cols = slice(q * width, (q + 1) * width)
        x = jnp.dot(placer, tok_ref[:, cols], preferred_element_type=jnp.float32)
        x_ref[:, cols] = x.astype(jnp.bfloat16)
        dy = jnp.dot(placer, cot_ref[:, cols], preferred_element_type=jnp.float32)
        dy_ref[:, cols] = (gate * dy).astype(jnp.bfloat16)
    fold = fold_ref[...]
    copies = [keep]
    for b in range(slot_count // LANES):
        out_ref[b] = fold_block(b, x_ref, dy_ref, fold)
        copies += start_all(
            [pltpu.make_async_copy(out_ref.at[b], send_hbm.at[b], out_sems.at[b])]
        )
    for copy in copies:
        copy.wait()


def expert_kernel(
    recv_hbm, ahead_hbm, back_hbm, unfold_hbm, fold_hbm,
    send_hbm, x_hbm, dy_hbm, hidden_hbm, paired_hbm,
    chunk_ref, ahead_ref, back_ref, unfold_ref, fold_ref,
    x_ref, dy_ref, hidden_ref, paired_ref, y_ref, dx_ref,
    recv_sems, load_sems, send_sems, keep_sems,
):
    blocks = chunk_ref.shape[0]
    feature_dim = x_ref.shape[1]
    units = hidden_ref.shape[1]
    pairs = [(unfold_hbm, unfold_ref)]
    pairs += [(ahead_hbm.at[i], ahead_ref.at[i]) for i in range(3)]
    pairs += [(back_hbm, back_ref), (fold_hbm, fold_ref)]
    loads = [
        pltpu.make_async_copy(src, dst, load_sems.at[i]) for i, (src, dst) in enumerate(pairs)
    ]
    loads[0].start()
    arrivals = start_all(
        [
            pltpu.make_async_copy(recv_hbm.at[b], chunk_ref.at[b], recv_sems.at[b])
            for b in range(blocks)
        ]
    )
    start_all(loads[1:])
    loads[0].wait()
    unfold = unfold_ref[...]
    for b in range(blocks):
        arrivals[b].wait()
        unfold_block(b, chunk_ref[b], unfold, x_ref, dy_ref)
    for copy in loads[1:4]:
        copy.wait()
    pre_gate = jnp.dot(x_ref[...], ahead_ref[0], preferred_element_type=jnp.float32)
    pre_up = jnp.dot(x_ref[...], ahead_ref[1], preferred_element_type=jnp.float32)
    hidden_grad = jnp.dot(dy_ref[...], ahead_ref[2], preferred_element_type=jnp.float32)
    gate_sig = jax.nn.sigmoid(pre_gate)
    gate_act = pre_gate * gate_sig
    hidden_ref[...] = (gate_act * pre_up).astype(jnp.bfloat16)
    gate_pre = hidden_grad * pre_up * gate_sig * (1.0 + pre_gate * (1.0 - gate_sig))
    paired_ref[:, :units] = gate_pre.astype(jnp.bfloat16)
    paired_ref[:, units:] = (hidden_grad * gate_act).astype(jnp.bfloat16)
    loads[4].wait()
    copies = start_all(
        [
            pltpu.make_async_copy(x_ref, x_hbm, keep_sems.at[0]),
            pltpu.make_async_copy(dy_ref, dy_hbm, keep_sems.at[1]),
            pltpu.make_async_copy(hidden_ref, hidden_hbm, keep_sems.at[2]),
            pltpu.make_async_copy(paired_ref, paired_hbm, keep_sems.at[3]),
        ]
    )
    width = feature_dim // QUARTERS
    for q in range(QUARTERS):
        cols = slice(q * width, (q + 1) * width)
        y = jnp.dot(
            hidden_ref[...], back_ref[2 * units :, cols], preferred_element_type=jnp.float32
        )
        y_ref[:, cols] = y.astype(jnp.bfloat16)
        dx = jnp.dot(
            paired_ref[...], back_ref[: 2 * units, cols], preferred_element_type=jnp.float32
        )
        dx_ref[:, cols] = dx.astype(jnp.bfloat16)
    loads[5].wait()
    fold = fold_ref[...]
    for b in range(blocks):
        chunk_ref[b] = fold_block(b, y_ref, dx_ref, fold)
        copies += start_all(
            [pltpu.make_async_copy(chunk_ref.at[b], send_hbm.at[b], send_sems.at[b])]
        )
    for copy in copies:
        copy.wait()


def finish_kernel(
    recv_ref, slots_ref, gates_ref, unfold_ref,
    outputs_hbm, grads_hbm,
    y_ref, dx_ref, outputs_ref, grads_ref, sems,
):
    blocks = recv_ref.shape[0]
    tok_rows, feature_dim = outputs_ref.shape
    slot_count = y_ref.shape[0]
    slot = lax.broadcasted_iota(jnp.int32, (tok_rows, slot_count), 1)
    hits = [slot == column(slots_ref[k : k + 1, :]) for k in range(2)]
    gates = [column(gates_ref[k : k + 1, :]) for k in range(2)]
    takers = [jnp.where(hit, 1.0, 0.0).astype(jnp.bfloat16) for hit in hits]
    both = jnp.where(hits[0] | hits[1], 1.0, 0.0).astype(jnp.bfloat16)
    unfold = unfold_ref[...]
    for b in range(blocks):
        unfold_block(b, recv_ref[b], unfold, y_ref, dx_ref)
    width = feature_dim // QUARTERS
    copies = []
    for q in range(QUARTERS):
        cols = slice(q * width, (q + 1) * width)
        total = sum(
            gates[k] * jnp.dot(takers[k], y_ref[:, cols], preferred_element_type=jnp.float32)
            for k in range(2)
        )
        outputs_ref[:, cols] = total.astype(jnp.bfloat16)
        grad = jnp.dot(both, dx_ref[:, cols], preferred_element_type=jnp.float32)
        grads_ref[:, cols] = grad.astype(jnp.bfloat16)
        copies += start_all(
            [
                pltpu.make_async_copy(
                    outputs_ref.at[:, cols], outputs_hbm.at[:, cols], sems.at[2 * q]
                ),
                pltpu.make_async_copy(
                    grads_ref.at[:, cols], grads_hbm.at[:, cols], sems.at[2 * q + 1]
                ),
            ]
        )
    for copy in copies:
        copy.wait()


def exchange(chunks, ep_count):
    width = chunks.shape[-1]
    moved = lax.all_to_all(
        chunks.reshape(ep_count, CHUNK, width), "ep", split_axis=0, concat_axis=0, tiled=True
    )
    return moved.reshape(chunks.shape)


def dp_partner(value, mask):
    pairs = [(source, source ^ mask) for source in range(lax.axis_size("dp"))]
    return lax.ppermute(value, "dp", pairs)


def body(tokens, cotangent, experts, gates, weights, swap_flags):
    ep_count = lax.axis_size("ep")
    half_ep = ep_count // 2
    tok_rows, feature_dim = tokens.shape
    slot_count = ep_count * CAP
    blocks = ep_count // GROUP
    units = weights.shape[3]
    width = feature_dim // QUARTERS
    my_index = lax.axis_index("ep")
    bf16 = jnp.bfloat16
    vmem = pl.BlockSpec(memory_space=pltpu.VMEM)
    hbm = pl.BlockSpec(memory_space=pltpu.HBM)
    dma = pltpu.SemaphoreType.DMA
    unfold = unfold_matrix()
    fold = jnp.asarray(unfold.T, bf16)
    unfold = jnp.asarray(unfold, bf16)
    chunks_shape = jax.ShapeDtypeStruct((blocks, BLOCK, width), bf16)
    rows_shape = jax.ShapeDtypeStruct((slot_count, feature_dim), bf16)
    tok_shape = jax.ShapeDtypeStruct((tok_rows, feature_dim), bf16)
    hidden_shape = jax.ShapeDtypeStruct((slot_count, units), bf16)
    paired_shape = jax.ShapeDtypeStruct((slot_count, 2 * units), bf16)
    slots_shape = jax.ShapeDtypeStruct((2, tok_rows), jnp.int32)

    def scratch(shape):
        return pltpu.VMEM(shape.shape, shape.dtype)

    gate_rows = gates.T
    send, slots = pl.pallas_call(
        prep_kernel,
        out_shape=(chunks_shape, slots_shape),
        in_specs=[hbm] * 6,
        out_specs=(hbm, hbm),
        scratch_shapes=[
            scratch(tok_shape),
            scratch(tok_shape),
            scratch(slots_shape),
            pltpu.VMEM((2, tok_rows), jnp.float32),
            pltpu.VMEM((1, half_ep), jnp.int32),
            pltpu.VMEM((BLOCK, BLOCK), bf16),
            scratch(slots_shape),
            scratch(rows_shape),
            scratch(rows_shape),
            scratch(chunks_shape),
            dma((6,)),
            dma((blocks,)),
            dma,
        ],
        compiler_params=pltpu.CompilerParams(vmem_limit_bytes=VMEM_MIB * MIB),
        name="prep",
    )(tokens, cotangent, experts.T, gate_rows, swap_flags.reshape(1, half_ep), fold)

    pair_lanes = jnp.arange(half_ep, dtype=jnp.int32)
    my_flag = jnp.sum(jnp.where(pair_lanes == my_index % half_ep, swap_flags, 0)) > 0
    own_weights = weights[0]
    swap_pairs = [(source, source ^ half_ep) for source in range(ep_count)]
    partner = lax.ppermute(own_weights, "ep", swap_pairs)
    own_weights = jnp.where(my_flag, partner, own_weights)
    dp_count = lax.axis_size("dp")
    my_dp = lax.axis_index("dp")
    shard_rows = feature_dim // dp_count
    full_weights = jnp.zeros((3, feature_dim, units), bf16)
    for mask in range(dp_count):
        shard = own_weights if mask == 0 else dp_partner(own_weights, mask)
        start = (my_dp ^ mask) * shard_rows
        full_weights = lax.dynamic_update_slice_in_dim(full_weights, shard, start, axis=1)
    back = full_weights.transpose(0, 2, 1).reshape(3 * units, feature_dim)

    recv = exchange(send, ep_count)

    send_back, rows_x, rows_dy, hidden, paired = pl.pallas_call(
        expert_kernel,
        out_shape=(chunks_shape, rows_shape, rows_shape, hidden_shape, paired_shape),
        in_specs=[hbm] * 5,
        out_specs=(hbm,) * 5,
        scratch_shapes=[
            scratch(chunks_shape),
            pltpu.VMEM((3, feature_dim, units), bf16),
            pltpu.VMEM((3 * units, feature_dim), bf16),
            pltpu.VMEM((BLOCK, BLOCK), bf16),
            pltpu.VMEM((BLOCK, BLOCK), bf16),
            scratch(rows_shape),
            scratch(rows_shape),
            scratch(hidden_shape),
            scratch(paired_shape),
            scratch(rows_shape),
            scratch(rows_shape),
            dma((blocks,)),
            dma((6,)),
            dma((blocks,)),
            dma((4,)),
        ],
        compiler_params=pltpu.CompilerParams(vmem_limit_bytes=EXPERT_MIB * MIB),
        name="expert",
    )(recv, full_weights, back, unfold, fold)

    recv_back = exchange(send_back, ep_count)

    pair_term = jnp.einsum("rc,rf->cf", rows_x, paired, preferred_element_type=jnp.float32)
    down_term = jnp.einsum("rd,rf->df", rows_dy, hidden, preferred_element_type=jnp.float32)
    terms = jnp.concatenate([pair_term.astype(bf16), down_term.astype(bf16)], axis=1)
    total = jnp.zeros((shard_rows, 3 * units), jnp.float32)
    for mask in range(dp_count):
        start = (my_dp ^ mask) * shard_rows
        shard = lax.dynamic_slice_in_dim(terms, start, shard_rows, 0)
        total += (shard if mask == 0 else dp_partner(shard, mask)).astype(jnp.float32)
    mine = total.astype(bf16)
    weight_grads = jnp.stack(
        [mine[:, :units], mine[:, units : 2 * units], mine[:, 2 * units :]]
    )[None]

    outputs, input_grads = pl.pallas_call(
        finish_kernel,
        out_shape=(tok_shape, tok_shape),
        in_specs=[vmem] * 4,
        out_specs=(hbm, hbm),
        scratch_shapes=[
            scratch(rows_shape),
            scratch(rows_shape),
            scratch(tok_shape),
            scratch(tok_shape),
            dma((2 * QUARTERS,)),
        ],
        compiler_params=pltpu.CompilerParams(vmem_limit_bytes=40 * MIB),
        name="finish",
    )(recv_back, slots, gate_rows, unfold)
    return (outputs, input_grads, weight_grads)


def solution(mesh):
    return jax.shard_map(
        body,
        mesh=mesh,
        in_specs=(
            P(("ep", "dp"), None),
            P(("ep", "dp"), None),
            P(("ep", "dp"), None),
            P(("ep", "dp"), None),
            P("ep", None, "dp", None),
            P(),
        ),
        out_specs=(P(("ep", "dp"), None), P(("ep", "dp"), None), P("ep", None, "dp", None)),
        check_vma=False,
    )
```

```python
import jax
import jax.numpy as jnp
import numpy as np
from jax import lax
from jax.experimental import pallas as pl
from jax.experimental.pallas import tpu as pltpu
from jax.sharding import PartitionSpec as P

CAP = 3
QUARTERS = 4
GROUP = 16
HALF = GROUP // 2
CHUNK = 2 * QUARTERS * CAP
BLOCK = GROUP * CHUNK
LANES = GROUP * CAP
MIB = 1 << 20
VMEM_MIB = 60
EXPERT_MIB = 107


def unfold_matrix():
    row = np.arange(HALF * CHUNK)
    piece, within = row // (HALF * CAP), row % (HALF * CAP)
    array, quarter = piece // QUARTERS, piece % QUARTERS
    peer, route = within // CAP, within % CAP
    source = peer * CHUNK + array * (CHUNK // 2) + quarter * CAP + route
    return (source[:, None] == row[None, :]).astype(np.float32)


def fold_block(block, first, second, fold):
    width = first.shape[1] // QUARTERS
    piece = HALF * CAP
    halves = []
    for start in (block * LANES, block * LANES + piece):
        parts = [
            ref[start : start + piece, q * width : (q + 1) * width]
            for ref in (first, second)
            for q in range(QUARTERS)
        ]
        stacked = jnp.concatenate(parts, axis=0).astype(jnp.bfloat16)
        folded = jnp.dot(fold, stacked, preferred_element_type=jnp.float32)
        halves.append(folded.astype(jnp.bfloat16))
    return jnp.concatenate(halves, axis=0)


def unfold_block(block, chunks, unfold, first, second):
    width = chunks.shape[1]
    piece = HALF * CAP
    rows = slice(block * LANES, (block + 1) * LANES)
    half = chunks.shape[0] // 2
    opened = [
        jnp.dot(unfold, part, preferred_element_type=jnp.float32)
        for part in (chunks[:half], chunks[half:])
    ]
    for index, ref in enumerate((first, second)):
        for q in range(QUARTERS):
            start = (index * QUARTERS + q) * piece
            both = jnp.concatenate([part[start : start + piece] for part in opened], axis=0)
            ref[rows, q * width : (q + 1) * width] = both.astype(jnp.bfloat16)


def column(row):
    n = row.shape[1]
    same = lax.broadcasted_iota(jnp.int32, (n, n), 0) == lax.broadcasted_iota(jnp.int32, (n, n), 1)
    return jnp.sum(jnp.where(same, row, jnp.zeros_like(row)), axis=1, keepdims=True)


def start_all(copies):
    for copy in copies:
        copy.start()
    return copies


def prep_kernel(
    tok_hbm, cot_hbm, experts_hbm, gates_hbm, flags_hbm, fold_hbm,
    send_hbm, slots_hbm,
    tok_ref, cot_ref, experts_ref, gates_ref, flags_ref, fold_ref, slots_ref, x_ref, dy_ref, out_ref,
    in_sems, out_sems, slot_sem,
):
    tok_rows, feature_dim = tok_ref.shape
    half = flags_ref.shape[1]
    slot_count = x_ref.shape[0]
    pairs = [
        (experts_hbm, experts_ref), (flags_hbm, flags_ref), (gates_hbm, gates_ref),
        (tok_hbm, tok_ref), (cot_hbm, cot_ref), (fold_hbm, fold_ref),
    ]
    loads = start_all(
        [pltpu.make_async_copy(src, dst, in_sems.at[i]) for i, (src, dst) in enumerate(pairs)]
    )
    loads[0].wait()
    loads[1].wait()
    flags = column(flags_ref[...])
    trow = []
    for k in range(2):
        row = experts_ref[k : k + 1, :]
        sub = lax.broadcasted_iota(jnp.int32, (half, tok_rows), 0)
        mine = jnp.sum(jnp.where((row & (half - 1)) == sub, flags, 0), axis=0, keepdims=True)
        trow.append(row ^ (mine * half))
    tcol = [column(row) for row in trow]
    sub = lax.broadcasted_iota(jnp.int32, (tok_rows, tok_rows), 0)
    lane = lax.broadcasted_iota(jnp.int32, (tok_rows, tok_rows), 1)
    slots = []
    for k in range(2):
        rank = jnp.zeros((1, tok_rows), jnp.int32)
        for j in range(2):
            hit = (tcol[j] == trow[k]) & (sub * 2 + j < lane * 2 + k)
            rank += jnp.sum(jnp.where(hit, 1, 0), axis=0, keepdims=True)
        slots.append(trow[k] * CAP + rank)
        slots_ref[k : k + 1, :] = slots[k]
    keep = pltpu.make_async_copy(slots_ref, slots_hbm, slot_sem)
    keep.start()
    slot = lax.broadcasted_iota(jnp.int32, (slot_count, tok_rows), 0)
    hits = [slot == slots[k] for k in range(2)]
    loads[2].wait()
    gate = sum(
        jnp.sum(jnp.where(hits[k], gates_ref[k : k + 1, :], 0.0), axis=1, keepdims=True)
        for k in range(2)
    )
    placer = jnp.where(hits[0] | hits[1], 1.0, 0.0).astype(jnp.bfloat16)
    for copy in loads[3:]:
        copy.wait()
    width = feature_dim // QUARTERS
    for q in range(QUARTERS):
        cols = slice(q * width, (q + 1) * width)
        x = jnp.dot(placer, tok_ref[:, cols], preferred_element_type=jnp.float32)
        x_ref[:, cols] = x
        dy = jnp.dot(placer, cot_ref[:, cols], preferred_element_type=jnp.float32)
        dy_ref[:, cols] = gate * dy
    fold = fold_ref[...]
    copies = [keep]
    for b in range(slot_count // LANES):
        out_ref[b] = fold_block(b, x_ref, dy_ref, fold)
        copies += start_all(
            [pltpu.make_async_copy(out_ref.at[b], send_hbm.at[b], out_sems.at[b])]
        )
    for copy in copies:
        copy.wait()


def expert_kernel(
    recv_hbm, ahead_hbm, back_hbm, unfold_hbm, fold_hbm,
    send_hbm, x_hbm, dy_hbm, hidden_hbm, paired_hbm,
    chunk_ref, ahead_ref, back_ref, unfold_ref, fold_ref,
    x_ref, dy_ref, hidden_ref, paired_ref, y_ref, dx_ref,
    recv_sems, load_sems, send_sems, keep_sems,
):
    blocks = chunk_ref.shape[0]
    feature_dim = x_ref.shape[1]
    units = hidden_ref.shape[1]
    pairs = [(unfold_hbm, unfold_ref)]
    pairs += [(ahead_hbm.at[i], ahead_ref.at[i]) for i in range(3)]
    pairs += [(back_hbm, back_ref), (fold_hbm, fold_ref)]
    loads = [
        pltpu.make_async_copy(src, dst, load_sems.at[i]) for i, (src, dst) in enumerate(pairs)
    ]
    loads[0].start()
    arrivals = start_all(
        [
            pltpu.make_async_copy(recv_hbm.at[b], chunk_ref.at[b], recv_sems.at[b])
            for b in range(blocks)
        ]
    )
    start_all(loads[1:])
    loads[0].wait()
    unfold = unfold_ref[...]
    for b in range(blocks):
        arrivals[b].wait()
        unfold_block(b, chunk_ref[b], unfold, x_ref, dy_ref)
    for copy in loads[1:4]:
        copy.wait()
    pre_gate = jnp.dot(x_ref[...], ahead_ref[0], preferred_element_type=jnp.float32)
    pre_up = jnp.dot(x_ref[...], ahead_ref[1], preferred_element_type=jnp.float32)
    hidden_grad = jnp.dot(dy_ref[...], ahead_ref[2], preferred_element_type=jnp.float32)
    gate_sig = jax.nn.sigmoid(pre_gate)
    gate_act = pre_gate * gate_sig
    hidden_ref[...] = (gate_act * pre_up).astype(jnp.bfloat16)
    gate_pre = hidden_grad * pre_up * gate_sig * (1.0 + pre_gate * (1.0 - gate_sig))
    paired_ref[:, :units] = gate_pre.astype(jnp.bfloat16)
    paired_ref[:, units:] = (hidden_grad * gate_act).astype(jnp.bfloat16)
    loads[4].wait()
    copies = start_all(
        [
            pltpu.make_async_copy(x_ref, x_hbm, keep_sems.at[0]),
            pltpu.make_async_copy(dy_ref, dy_hbm, keep_sems.at[1]),
            pltpu.make_async_copy(hidden_ref, hidden_hbm, keep_sems.at[2]),
            pltpu.make_async_copy(paired_ref, paired_hbm, keep_sems.at[3]),
        ]
    )
    width = feature_dim // QUARTERS
    for q in range(QUARTERS):
        cols = slice(q * width, (q + 1) * width)
        y = jnp.dot(
            hidden_ref[...], back_ref[2 * units :, cols], preferred_element_type=jnp.float32
        )
        y_ref[:, cols] = y
        dx = jnp.dot(
            paired_ref[...], back_ref[: 2 * units, cols], preferred_element_type=jnp.float32
        )
        dx_ref[:, cols] = dx
    loads[5].wait()
    fold = fold_ref[...]
    for b in range(blocks):
        chunk_ref[b] = fold_block(b, y_ref, dx_ref, fold)
        copies += start_all(
            [pltpu.make_async_copy(chunk_ref.at[b], send_hbm.at[b], send_sems.at[b])]
        )
    for copy in copies:
        copy.wait()


def finish_kernel(
    recv_ref, slots_ref, gates_ref, unfold_ref,
    outputs_hbm, grads_hbm,
    y_ref, dx_ref, outputs_ref, grads_ref, sems,
):
    blocks = recv_ref.shape[0]
    tok_rows, feature_dim = outputs_ref.shape
    slot_count = y_ref.shape[0]
    slot = lax.broadcasted_iota(jnp.int32, (tok_rows, slot_count), 1)
    hits = [slot == column(slots_ref[k : k + 1, :]) for k in range(2)]
    gates = [column(gates_ref[k : k + 1, :]) for k in range(2)]
    takers = [jnp.where(hit, 1.0, 0.0).astype(jnp.bfloat16) for hit in hits]
    both = jnp.where(hits[0] | hits[1], 1.0, 0.0).astype(jnp.bfloat16)
    unfold = unfold_ref[...]
    for b in range(blocks):
        unfold_block(b, recv_ref[b], unfold, y_ref, dx_ref)
    width = feature_dim // QUARTERS
    copies = []
    for q in range(QUARTERS):
        cols = slice(q * width, (q + 1) * width)
        total = sum(
            gates[k] * jnp.dot(takers[k], y_ref[:, cols], preferred_element_type=jnp.float32)
            for k in range(2)
        )
        outputs_ref[:, cols] = total.astype(jnp.bfloat16)
        grad = jnp.dot(both, dx_ref[:, cols], preferred_element_type=jnp.float32)
        grads_ref[:, cols] = grad.astype(jnp.bfloat16)
        copies += start_all(
            [
                pltpu.make_async_copy(
                    outputs_ref.at[:, cols], outputs_hbm.at[:, cols], sems.at[2 * q]
                ),
                pltpu.make_async_copy(
                    grads_ref.at[:, cols], grads_hbm.at[:, cols], sems.at[2 * q + 1]
                ),
            ]
        )
    for copy in copies:
        copy.wait()


def exchange(chunks, ep_count):
    width = chunks.shape[-1]
    moved = lax.all_to_all(
        chunks.reshape(ep_count, CHUNK, width), "ep", split_axis=0, concat_axis=0, tiled=True
    )
    return moved.reshape(chunks.shape)


def dp_partner(value, mask):
    pairs = [(source, source ^ mask) for source in range(lax.axis_size("dp"))]
    return lax.ppermute(value, "dp", pairs)


def body(tokens, cotangent, experts, gates, weights, swap_flags):
    ep_count = lax.axis_size("ep")
    half_ep = ep_count // 2
    tok_rows, feature_dim = tokens.shape
    slot_count = ep_count * CAP
    blocks = ep_count // GROUP
    units = weights.shape[3]
    width = feature_dim // QUARTERS
    my_index = lax.axis_index("ep")
    bf16 = jnp.bfloat16
    vmem = pl.BlockSpec(memory_space=pltpu.VMEM)
    hbm = pl.BlockSpec(memory_space=pltpu.HBM)
    dma = pltpu.SemaphoreType.DMA
    unfold = unfold_matrix()
    fold = jnp.asarray(unfold.T, bf16)
    unfold = jnp.asarray(unfold, bf16)
    chunks_shape = jax.ShapeDtypeStruct((blocks, BLOCK, width), bf16)
    rows_shape = jax.ShapeDtypeStruct((slot_count, feature_dim), bf16)
    tok_shape = jax.ShapeDtypeStruct((tok_rows, feature_dim), bf16)
    hidden_shape = jax.ShapeDtypeStruct((slot_count, units), bf16)
    paired_shape = jax.ShapeDtypeStruct((slot_count, 2 * units), bf16)
    slots_shape = jax.ShapeDtypeStruct((2, tok_rows), jnp.int32)

    wide_vmem = pltpu.VMEM(rows_shape.shape, jnp.float32)
    fold_vmem = pltpu.VMEM(fold.shape, bf16)

    def scratch(shape):
        return pltpu.VMEM(shape.shape, shape.dtype)

    gate_rows = gates.T
    send, slots = pl.pallas_call(
        prep_kernel,
        out_shape=(chunks_shape, slots_shape),
        in_specs=[hbm] * 6,
        out_specs=(hbm, hbm),
        scratch_shapes=[
            scratch(tok_shape),
            scratch(tok_shape),
            scratch(slots_shape),
            pltpu.VMEM((2, tok_rows), jnp.float32),
            pltpu.VMEM((1, half_ep), jnp.int32),
            fold_vmem,
            scratch(slots_shape),
            wide_vmem,
            wide_vmem,
            scratch(chunks_shape),
            dma((6,)),
            dma((blocks,)),
            dma,
        ],
        compiler_params=pltpu.CompilerParams(vmem_limit_bytes=VMEM_MIB * MIB),
        name="prep",
    )(tokens, cotangent, experts.T, gate_rows, swap_flags.reshape(1, half_ep), fold)

    pair_lanes = jnp.arange(half_ep, dtype=jnp.int32)
    my_flag = jnp.sum(jnp.where(pair_lanes == my_index % half_ep, swap_flags, 0)) > 0
    own_weights = weights[0]
    swap_pairs = [(source, source ^ half_ep) for source in range(ep_count)]
    partner = lax.ppermute(own_weights, "ep", swap_pairs)
    own_weights = jnp.where(my_flag, partner, own_weights)
    dp_count = lax.axis_size("dp")
    my_dp = lax.axis_index("dp")
    shard_rows = feature_dim // dp_count
    full_weights = jnp.zeros((3, feature_dim, units), bf16)
    for mask in range(dp_count):
        shard = own_weights if mask == 0 else dp_partner(own_weights, mask)
        start = (my_dp ^ mask) * shard_rows
        full_weights = lax.dynamic_update_slice_in_dim(full_weights, shard, start, axis=1)
    back = full_weights.transpose(0, 2, 1).reshape(3 * units, feature_dim)

    recv = exchange(send, ep_count)

    send_back, rows_x, rows_dy, hidden, paired = pl.pallas_call(
        expert_kernel,
        out_shape=(chunks_shape, rows_shape, rows_shape, hidden_shape, paired_shape),
        in_specs=[hbm] * 5,
        out_specs=(hbm,) * 5,
        scratch_shapes=[
            scratch(chunks_shape),
            pltpu.VMEM((3, feature_dim, units), bf16),
            pltpu.VMEM((3 * units, feature_dim), bf16),
            fold_vmem,
            fold_vmem,
            scratch(rows_shape),
            scratch(rows_shape),
            scratch(hidden_shape),
            scratch(paired_shape),
            wide_vmem,
            wide_vmem,
            dma((blocks,)),
            dma((6,)),
            dma((blocks,)),
            dma((4,)),
        ],
        compiler_params=pltpu.CompilerParams(vmem_limit_bytes=EXPERT_MIB * (MIB // 2)),
        name="expert",
    )(recv, full_weights, back, unfold, fold)

    recv_back = exchange(send_back, ep_count)

    pair_term = jnp.einsum("rc,rf->cf", rows_x, paired, preferred_element_type=jnp.float32)
    down_term = jnp.einsum("rd,rf->df", rows_dy, hidden, preferred_element_type=jnp.float32)
    terms = jnp.concatenate([pair_term.astype(bf16), down_term.astype(bf16)], axis=1)
    total = jnp.zeros((shard_rows, 3 * units), jnp.float32)
    for mask in range(dp_count):
        start = (my_dp ^ mask) * shard_rows
        shard = lax.dynamic_slice_in_dim(terms, start, shard_rows, 0)
        total += (shard if mask == 0 else dp_partner(shard, mask)).astype(jnp.float32)
    mine = total.astype(bf16)
    weight_grads = jnp.stack(
        [mine[:, :units], mine[:, units : 2 * units], mine[:, 2 * units :]]
    )[None]

    outputs, input_grads = pl.pallas_call(
        finish_kernel,
        out_shape=(tok_shape, tok_shape),
        in_specs=[vmem] * 4,
        out_specs=(hbm, hbm),
        scratch_shapes=[
            scratch(rows_shape),
            scratch(rows_shape),
            scratch(tok_shape),
            scratch(tok_shape),
            dma((2 * QUARTERS,)),
        ],
        compiler_params=pltpu.CompilerParams(vmem_limit_bytes=40 * MIB),
        name="finish",
    )(recv_back, slots, gate_rows, unfold)
    return (outputs, input_grads, weight_grads)


def solution(mesh):
    return jax.shard_map(
        body,
        mesh=mesh,
        in_specs=(
            P(("ep", "dp"), None),
            P(("ep", "dp"), None),
            P(("ep", "dp"), None),
            P(("ep", "dp"), None),
            P("ep", None, "dp", None),
            P(),
        ),
        out_specs=(P(("ep", "dp"), None), P(("ep", "dp"), None), P("ep", None, "dp", None)),
        check_vma=False,
    )
```

```python
import jax
import jax.numpy as jnp
import numpy as np
from jax import lax
from jax.experimental import pallas as pl
from jax.experimental.pallas import tpu as pltpu
from jax.sharding import PartitionSpec as P

CAP = 3
QUARTERS = 4
GROUP = 16
HALF = GROUP // 2
CHUNK = 2 * QUARTERS * CAP
BLOCK = GROUP * CHUNK
LANES = GROUP * CAP
MIB = 1 << 20
VMEM_MIB = 60
EXPERT_MIB = 36
GRADS_MIB = 24


def unfold_matrix():
    row = np.arange(HALF * CHUNK)
    piece, within = row // (HALF * CAP), row % (HALF * CAP)
    array, quarter = piece // QUARTERS, piece % QUARTERS
    peer, route = within // CAP, within % CAP
    source = peer * CHUNK + array * (CHUNK // 2) + quarter * CAP + route
    return (source[:, None] == row[None, :]).astype(np.float32)


def fold_block(block, first, second, fold):
    width = first.shape[1] // QUARTERS
    piece = HALF * CAP
    halves = []
    for start in (block * LANES, block * LANES + piece):
        parts = [
            ref[start : start + piece, q * width : (q + 1) * width]
            for ref in (first, second)
            for q in range(QUARTERS)
        ]
        stacked = jnp.concatenate(parts, axis=0).astype(jnp.bfloat16)
        folded = jnp.dot(fold, stacked, preferred_element_type=jnp.float32)
        halves.append(folded.astype(jnp.bfloat16))
    return jnp.concatenate(halves, axis=0)


def unfold_block(block, chunks, unfold, first, second):
    width = chunks.shape[1]
    piece = HALF * CAP
    rows = slice(block * LANES, (block + 1) * LANES)
    half = chunks.shape[0] // 2
    opened = [
        jnp.dot(unfold, part, preferred_element_type=jnp.float32)
        for part in (chunks[:half], chunks[half:])
    ]
    for index, ref in enumerate((first, second)):
        for q in range(QUARTERS):
            start = (index * QUARTERS + q) * piece
            both = jnp.concatenate([part[start : start + piece] for part in opened], axis=0)
            ref[rows, q * width : (q + 1) * width] = both.astype(jnp.bfloat16)


def column(row):
    n = row.shape[1]
    same = lax.broadcasted_iota(jnp.int32, (n, n), 0) == lax.broadcasted_iota(jnp.int32, (n, n), 1)
    return jnp.sum(jnp.where(same, row, jnp.zeros_like(row)), axis=1, keepdims=True)


def start_all(copies):
    for copy in copies:
        copy.start()
    return copies


def prep_kernel(
    tok_hbm, cot_hbm, experts_hbm, gates_hbm, flags_hbm, fold_hbm,
    send_hbm, slots_hbm,
    tok_ref, cot_ref, experts_ref, gates_ref, flags_ref, fold_ref, slots_ref, x_ref, dy_ref, out_ref,
    in_sems, out_sems, slot_sem,
):
    tok_rows, feature_dim = tok_ref.shape
    half = flags_ref.shape[1]
    slot_count = x_ref.shape[0]
    pairs = [
        (experts_hbm, experts_ref), (flags_hbm, flags_ref), (gates_hbm, gates_ref),
        (tok_hbm, tok_ref), (cot_hbm, cot_ref), (fold_hbm, fold_ref),
    ]
    loads = start_all(
        [pltpu.make_async_copy(src, dst, in_sems.at[i]) for i, (src, dst) in enumerate(pairs)]
    )
    loads[0].wait()
    loads[1].wait()
    flags = column(flags_ref[...])
    trow = []
    for k in range(2):
        row = experts_ref[k : k + 1, :]
        sub = lax.broadcasted_iota(jnp.int32, (half, tok_rows), 0)
        mine = jnp.sum(jnp.where((row & (half - 1)) == sub, flags, 0), axis=0, keepdims=True)
        trow.append(row ^ (mine * half))
    tcol = [column(row) for row in trow]
    sub = lax.broadcasted_iota(jnp.int32, (tok_rows, tok_rows), 0)
    lane = lax.broadcasted_iota(jnp.int32, (tok_rows, tok_rows), 1)
    slots = []
    for k in range(2):
        rank = jnp.zeros((1, tok_rows), jnp.int32)
        for j in range(2):
            hit = (tcol[j] == trow[k]) & (sub * 2 + j < lane * 2 + k)
            rank += jnp.sum(jnp.where(hit, 1, 0), axis=0, keepdims=True)
        slots.append(trow[k] * CAP + rank)
        slots_ref[k : k + 1, :] = slots[k]
    keep = pltpu.make_async_copy(slots_ref, slots_hbm, slot_sem)
    keep.start()
    slot = lax.broadcasted_iota(jnp.int32, (slot_count, tok_rows), 0)
    hits = [slot == slots[k] for k in range(2)]
    loads[2].wait()
    gate = sum(
        jnp.sum(jnp.where(hits[k], gates_ref[k : k + 1, :], 0.0), axis=1, keepdims=True)
        for k in range(2)
    )
    placer = jnp.where(hits[0] | hits[1], 1.0, 0.0).astype(jnp.bfloat16)
    for copy in loads[3:]:
        copy.wait()
    width = feature_dim // QUARTERS
    for q in range(QUARTERS):
        cols = slice(q * width, (q + 1) * width)
        x = jnp.dot(placer, tok_ref[:, cols], preferred_element_type=jnp.float32)
        x_ref[:, cols] = x
        dy = jnp.dot(placer, cot_ref[:, cols], preferred_element_type=jnp.float32)
        dy_ref[:, cols] = gate * dy
    fold = fold_ref[...]
    copies = [keep]
    for b in range(slot_count // LANES):
        out_ref[b] = fold_block(b, x_ref, dy_ref, fold)
        copies += start_all(
            [pltpu.make_async_copy(out_ref.at[b], send_hbm.at[b], out_sems.at[b])]
        )
    for copy in copies:
        copy.wait()


def hidden_units(x_ref, dy_ref, w_ref, hidden_ref, paired_ref):
    units = hidden_ref.shape[1]
    pre_gate = jnp.dot(x_ref[...], w_ref[0], preferred_element_type=jnp.float32)
    pre_up = jnp.dot(x_ref[...], w_ref[1], preferred_element_type=jnp.float32)
    hidden_grad = jnp.dot(dy_ref[...], w_ref[2], preferred_element_type=jnp.float32)
    gate_sig = jax.nn.sigmoid(pre_gate)
    gate_act = pre_gate * gate_sig
    hidden_ref[...] = (gate_act * pre_up).astype(jnp.bfloat16)
    gate_pre = hidden_grad * pre_up * gate_sig * (1.0 + pre_gate * (1.0 - gate_sig))
    paired_ref[:, :units] = gate_pre.astype(jnp.bfloat16)
    paired_ref[:, units:] = (hidden_grad * gate_act).astype(jnp.bfloat16)


def expert_kernel(
    recv_ref, ahead_hbm, back_hbm, unfold_hbm, fold_hbm,
    send_ref,
    ahead_ref, back_ref, unfold_ref, fold_ref,
    x_ref, dy_ref, hidden_ref, paired_ref, y_ref, dx_ref,
    load_sems,
):
    blocks = recv_ref.shape[0]
    feature_dim = x_ref.shape[1]
    units = hidden_ref.shape[1]
    pairs = [(unfold_hbm, unfold_ref)]
    pairs += [(ahead_hbm.at[i], ahead_ref.at[i]) for i in range(3)]
    pairs += [(back_hbm, back_ref), (fold_hbm, fold_ref)]
    loads = [
        pltpu.make_async_copy(src, dst, load_sems.at[i]) for i, (src, dst) in enumerate(pairs)
    ]
    loads[0].start()
    start_all(loads[1:])
    loads[0].wait()
    unfold = unfold_ref[...]
    for b in range(blocks):
        unfold_block(b, recv_ref[b], unfold, x_ref, dy_ref)
    for copy in loads[1:4]:
        copy.wait()
    hidden_units(x_ref, dy_ref, ahead_ref, hidden_ref, paired_ref)
    loads[4].wait()
    width = feature_dim // QUARTERS
    for q in range(QUARTERS):
        cols = slice(q * width, (q + 1) * width)
        y = jnp.dot(
            hidden_ref[...], back_ref[2 * units :, cols], preferred_element_type=jnp.float32
        )
        y_ref[:, cols] = y
        dx = jnp.dot(
            paired_ref[...], back_ref[: 2 * units, cols], preferred_element_type=jnp.float32
        )
        dx_ref[:, cols] = dx
    loads[5].wait()
    fold = fold_ref[...]
    for b in range(blocks):
        send_ref[b] = fold_block(b, y_ref, dx_ref, fold)


def grads_kernel(
    recv_hbm, w_hbm, unfold_hbm,
    terms_hbm,
    chunk_ref, w_ref, unfold_ref, x_ref, dy_ref, hidden_ref, paired_ref, terms_ref, load_sems, out_sems,
):
    units = hidden_ref.shape[1]
    pairs = [(recv_hbm, chunk_ref), (w_hbm, w_ref), (unfold_hbm, unfold_ref)]
    loads = start_all(
        [pltpu.make_async_copy(src, dst, load_sems.at[i]) for i, (src, dst) in enumerate(pairs)]
    )
    for copy in loads:
        copy.wait()
    for b in range(chunk_ref.shape[0]):
        unfold_block(b, chunk_ref[b], unfold_ref[...], x_ref, dy_ref)
    hidden_units(x_ref, dy_ref, w_ref, hidden_ref, paired_ref)
    width = x_ref.shape[1] // QUARTERS
    over_rows = (((0,), (0,)), ((), ()))
    copies = []
    for q in range(QUARTERS):
        cols = slice(q * width, (q + 1) * width)
        pair = lax.dot_general(
            x_ref[:, cols], paired_ref[...], over_rows, preferred_element_type=jnp.float32
        )
        terms_ref[cols, : 2 * units] = pair.astype(jnp.bfloat16)
        down = lax.dot_general(
            dy_ref[:, cols], hidden_ref[...], over_rows, preferred_element_type=jnp.float32
        )
        terms_ref[cols, 2 * units :] = down.astype(jnp.bfloat16)
        copies += start_all(
            [pltpu.make_async_copy(terms_ref.at[cols], terms_hbm.at[cols], out_sems.at[q])]
        )
    for copy in copies:
        copy.wait()


def finish_kernel(
    recv_ref, slots_ref, gates_ref, unfold_ref,
    outputs_hbm, grads_hbm,
    y_ref, dx_ref, outputs_ref, grads_ref, sems,
):
    blocks = recv_ref.shape[0]
    tok_rows, feature_dim = outputs_ref.shape
    slot_count = y_ref.shape[0]
    slot = lax.broadcasted_iota(jnp.int32, (tok_rows, slot_count), 1)
    hits = [slot == column(slots_ref[k : k + 1, :]) for k in range(2)]
    gates = [column(gates_ref[k : k + 1, :]) for k in range(2)]
    takers = [jnp.where(hit, 1.0, 0.0).astype(jnp.bfloat16) for hit in hits]
    both = jnp.where(hits[0] | hits[1], 1.0, 0.0).astype(jnp.bfloat16)
    unfold = unfold_ref[...]
    for b in range(blocks):
        unfold_block(b, recv_ref[b], unfold, y_ref, dx_ref)
    width = feature_dim // QUARTERS
    copies = []
    for q in range(QUARTERS):
        cols = slice(q * width, (q + 1) * width)
        total = sum(
            gates[k] * jnp.dot(takers[k], y_ref[:, cols], preferred_element_type=jnp.float32)
            for k in range(2)
        )
        outputs_ref[:, cols] = total.astype(jnp.bfloat16)
        grad = jnp.dot(both, dx_ref[:, cols], preferred_element_type=jnp.float32)
        grads_ref[:, cols] = grad.astype(jnp.bfloat16)
        copies += start_all(
            [
                pltpu.make_async_copy(
                    outputs_ref.at[:, cols], outputs_hbm.at[:, cols], sems.at[2 * q]
                ),
                pltpu.make_async_copy(
                    grads_ref.at[:, cols], grads_hbm.at[:, cols], sems.at[2 * q + 1]
                ),
            ]
        )
    for copy in copies:
        copy.wait()


def exchange(chunks, ep_count):
    width = chunks.shape[-1]
    moved = lax.all_to_all(
        chunks.reshape(ep_count, CHUNK, width), "ep", split_axis=0, concat_axis=0, tiled=True
    )
    return moved.reshape(chunks.shape)


def dp_partner(value, mask):
    pairs = [(source, source ^ mask) for source in range(lax.axis_size("dp"))]
    return lax.ppermute(value, "dp", pairs)


def body(tokens, cotangent, experts, gates, weights, swap_flags):
    ep_count = lax.axis_size("ep")
    half_ep = ep_count // 2
    tok_rows, feature_dim = tokens.shape
    slot_count = ep_count * CAP
    blocks = ep_count // GROUP
    units = weights.shape[3]
    width = feature_dim // QUARTERS
    my_index = lax.axis_index("ep")
    bf16 = jnp.bfloat16
    vmem = pl.BlockSpec(memory_space=pltpu.VMEM)
    hbm = pl.BlockSpec(memory_space=pltpu.HBM)
    dma = pltpu.SemaphoreType.DMA
    unfold = unfold_matrix()
    fold = jnp.asarray(unfold.T, bf16)
    unfold = jnp.asarray(unfold, bf16)
    chunks_shape = jax.ShapeDtypeStruct((blocks, BLOCK, width), bf16)
    rows_shape = jax.ShapeDtypeStruct((slot_count, feature_dim), bf16)
    tok_shape = jax.ShapeDtypeStruct((tok_rows, feature_dim), bf16)
    hidden_shape = jax.ShapeDtypeStruct((slot_count, units), bf16)
    paired_shape = jax.ShapeDtypeStruct((slot_count, 2 * units), bf16)
    slots_shape = jax.ShapeDtypeStruct((2, tok_rows), jnp.int32)

    wide_vmem = pltpu.VMEM(rows_shape.shape, jnp.float32)
    fold_vmem = pltpu.VMEM(fold.shape, bf16)

    def scratch(shape):
        return pltpu.VMEM(shape.shape, shape.dtype)

    gate_rows = gates.T
    send, slots = pl.pallas_call(
        prep_kernel,
        out_shape=(chunks_shape, slots_shape),
        in_specs=[hbm] * 6,
        out_specs=(hbm, hbm),
        scratch_shapes=[
            scratch(tok_shape),
            scratch(tok_shape),
            scratch(slots_shape),
            pltpu.VMEM((2, tok_rows), jnp.float32),
            pltpu.VMEM((1, half_ep), jnp.int32),
            fold_vmem,
            scratch(slots_shape),
            wide_vmem,
            wide_vmem,
            scratch(chunks_shape),
            dma((6,)),
            dma((blocks,)),
            dma,
        ],
        compiler_params=pltpu.CompilerParams(vmem_limit_bytes=VMEM_MIB * MIB),
        name="prep",
    )(tokens, cotangent, experts.T, gate_rows, swap_flags.reshape(1, half_ep), fold)

    pair_lanes = jnp.arange(half_ep, dtype=jnp.int32)
    my_flag = jnp.sum(jnp.where(pair_lanes == my_index % half_ep, swap_flags, 0)) > 0
    own_weights = weights[0]
    swap_pairs = [(source, source ^ half_ep) for source in range(ep_count)]
    partner = lax.ppermute(own_weights, "ep", swap_pairs)
    own_weights = jnp.where(my_flag, partner, own_weights)
    dp_count = lax.axis_size("dp")
    my_dp = lax.axis_index("dp")
    shard_rows = feature_dim // dp_count
    full_weights = jnp.zeros((3, feature_dim, units), bf16)
    for mask in range(dp_count):
        shard = own_weights if mask == 0 else dp_partner(own_weights, mask)
        start = (my_dp ^ mask) * shard_rows
        full_weights = lax.dynamic_update_slice_in_dim(full_weights, shard, start, axis=1)
    back = full_weights.transpose(0, 2, 1).reshape(3 * units, feature_dim)

    recv = exchange(send, ep_count)

    send_back = pl.pallas_call(
        expert_kernel,
        out_shape=chunks_shape,
        in_specs=[vmem] + [hbm] * 4,
        out_specs=vmem,
        scratch_shapes=[
            pltpu.VMEM((3, feature_dim, units), bf16),
            pltpu.VMEM((3 * units, feature_dim), bf16),
            fold_vmem,
            fold_vmem,
            scratch(rows_shape),
            scratch(rows_shape),
            scratch(hidden_shape),
            scratch(paired_shape),
            wide_vmem,
            wide_vmem,
            dma((6,)),
        ],
        compiler_params=pltpu.CompilerParams(vmem_limit_bytes=EXPERT_MIB * MIB),
        name="expert",
    )(recv, full_weights, back, unfold, fold)

    recv_back = exchange(send_back, ep_count)

    terms_shape = jax.ShapeDtypeStruct((feature_dim, 3 * units), bf16)
    terms = pl.pallas_call(
        grads_kernel,
        out_shape=terms_shape,
        in_specs=[hbm] * 3,
        out_specs=hbm,
        scratch_shapes=[
            scratch(chunks_shape),
            pltpu.VMEM((3, feature_dim, units), bf16),
            fold_vmem,
            scratch(rows_shape),
            scratch(rows_shape),
            scratch(hidden_shape),
            scratch(paired_shape),
            scratch(terms_shape),
            dma((3,)),
            dma((QUARTERS,)),
        ],
        compiler_params=pltpu.CompilerParams(vmem_limit_bytes=GRADS_MIB * MIB),
        name="grads",
    )(recv, full_weights, unfold)
    total = jnp.zeros((shard_rows, 3 * units), jnp.float32)
    for mask in range(dp_count):
        start = (my_dp ^ mask) * shard_rows
        shard = lax.dynamic_slice_in_dim(terms, start, shard_rows, 0)
        total += (shard if mask == 0 else dp_partner(shard, mask)).astype(jnp.float32)
    mine = total.astype(bf16)
    weight_grads = jnp.stack(
        [mine[:, :units], mine[:, units : 2 * units], mine[:, 2 * units :]]
    )[None]

    outputs, input_grads = pl.pallas_call(
        finish_kernel,
        out_shape=(tok_shape, tok_shape),
        in_specs=[vmem] * 4,
        out_specs=(hbm, hbm),
        scratch_shapes=[
            scratch(rows_shape),
            scratch(rows_shape),
            scratch(tok_shape),
            scratch(tok_shape),
            dma((2 * QUARTERS,)),
        ],
        compiler_params=pltpu.CompilerParams(vmem_limit_bytes=40 * MIB),
        name="finish",
    )(recv_back, slots, gate_rows, unfold)
    return (outputs, input_grads, weight_grads)


def solution(mesh):
    return jax.shard_map(
        body,
        mesh=mesh,
        in_specs=(
            P(("ep", "dp"), None),
            P(("ep", "dp"), None),
            P(("ep", "dp"), None),
            P(("ep", "dp"), None),
            P("ep", None, "dp", None),
            P(),
        ),
        out_specs=(P(("ep", "dp"), None), P(("ep", "dp"), None), P("ep", None, "dp", None)),
        check_vma=False,
    )
```

```python
import jax
import jax.numpy as jnp
import numpy as np
from jax import lax
from jax.experimental import pallas as pl
from jax.experimental.pallas import tpu as pltpu
from jax.sharding import PartitionSpec as P

CAP = 3
QUARTERS = 4
GROUP = 16
HALF = GROUP // 2
CHUNK = 2 * QUARTERS * CAP
BLOCK = GROUP * CHUNK
LANES = GROUP * CAP
MIB = 1 << 20
VMEM_MIB = 60
EXPERT_MIB = 44
GRADS_MIB = 28


def unfold_matrix():
    row = np.arange(HALF * CHUNK)
    piece, within = row // (HALF * CAP), row % (HALF * CAP)
    array, quarter = piece // QUARTERS, piece % QUARTERS
    peer, route = within // CAP, within % CAP
    source = peer * CHUNK + array * (CHUNK // 2) + quarter * CAP + route
    return (source[:, None] == row[None, :]).astype(np.float32)


def fold_block(block, first, second, fold):
    width = first.shape[1] // QUARTERS
    piece = HALF * CAP
    halves = []
    for start in (block * LANES, block * LANES + piece):
        parts = [
            ref[start : start + piece, q * width : (q + 1) * width]
            for ref in (first, second)
            for q in range(QUARTERS)
        ]
        stacked = jnp.concatenate(parts, axis=0).astype(jnp.bfloat16)
        folded = jnp.dot(fold, stacked, preferred_element_type=jnp.float32)
        halves.append(folded.astype(jnp.bfloat16))
    return jnp.concatenate(halves, axis=0)


def unfold_block(block, chunks, unfold, first, second):
    width = chunks.shape[1]
    piece = HALF * CAP
    rows = slice(block * LANES, (block + 1) * LANES)
    half = chunks.shape[0] // 2
    opened = [
        jnp.dot(unfold, part, preferred_element_type=jnp.float32)
        for part in (chunks[:half], chunks[half:])
    ]
    for index, ref in enumerate((first, second)):
        for q in range(QUARTERS):
            start = (index * QUARTERS + q) * piece
            both = jnp.concatenate([part[start : start + piece] for part in opened], axis=0)
            ref[rows, q * width : (q + 1) * width] = both.astype(jnp.bfloat16)


def column(row):
    n = row.shape[1]
    same = lax.broadcasted_iota(jnp.int32, (n, n), 0) == lax.broadcasted_iota(jnp.int32, (n, n), 1)
    return jnp.sum(jnp.where(same, row, jnp.zeros_like(row)), axis=1, keepdims=True)


def start_all(copies):
    for copy in copies:
        copy.start()
    return copies


def prep_kernel(
    tok_hbm, cot_hbm, experts_hbm, gates_hbm, flags_hbm, fold_hbm,
    send_hbm, slots_hbm,
    tok_ref, cot_ref, experts_ref, gates_ref, flags_ref, fold_ref, slots_ref, x_ref, dy_ref, out_ref,
    in_sems, out_sems, slot_sem,
):
    tok_rows, feature_dim = tok_ref.shape
    half = flags_ref.shape[1]
    slot_count = x_ref.shape[0]
    pairs = [
        (experts_hbm, experts_ref), (flags_hbm, flags_ref), (gates_hbm, gates_ref),
        (tok_hbm, tok_ref), (cot_hbm, cot_ref), (fold_hbm, fold_ref),
    ]
    loads = start_all(
        [pltpu.make_async_copy(src, dst, in_sems.at[i]) for i, (src, dst) in enumerate(pairs)]
    )
    loads[0].wait()
    loads[1].wait()
    flags = column(flags_ref[...])
    trow = []
    for k in range(2):
        row = experts_ref[k : k + 1, :]
        sub = lax.broadcasted_iota(jnp.int32, (half, tok_rows), 0)
        mine = jnp.sum(jnp.where((row & (half - 1)) == sub, flags, 0), axis=0, keepdims=True)
        trow.append(row ^ (mine * half))
    tcol = [column(row) for row in trow]
    sub = lax.broadcasted_iota(jnp.int32, (tok_rows, tok_rows), 0)
    lane = lax.broadcasted_iota(jnp.int32, (tok_rows, tok_rows), 1)
    slots = []
    for k in range(2):
        rank = jnp.zeros((1, tok_rows), jnp.int32)
        for j in range(2):
            hit = (tcol[j] == trow[k]) & (sub * 2 + j < lane * 2 + k)
            rank += jnp.sum(jnp.where(hit, 1, 0), axis=0, keepdims=True)
        slots.append(trow[k] * CAP + rank)
        slots_ref[k : k + 1, :] = slots[k]
    keep = pltpu.make_async_copy(slots_ref, slots_hbm, slot_sem)
    keep.start()
    slot = lax.broadcasted_iota(jnp.int32, (slot_count, tok_rows), 0)
    hits = [slot == slots[k] for k in range(2)]
    loads[2].wait()
    gate = sum(
        jnp.sum(jnp.where(hits[k], gates_ref[k : k + 1, :], 0.0), axis=1, keepdims=True)
        for k in range(2)
    )
    placer = jnp.where(hits[0] | hits[1], 1.0, 0.0).astype(jnp.bfloat16)
    for copy in loads[3:]:
        copy.wait()
    width = feature_dim // QUARTERS
    for q in range(QUARTERS):
        cols = slice(q * width, (q + 1) * width)
        x = jnp.dot(placer, tok_ref[:, cols], preferred_element_type=jnp.float32)
        x_ref[:, cols] = x
        dy = jnp.dot(placer, cot_ref[:, cols], preferred_element_type=jnp.float32)
        dy_ref[:, cols] = gate * dy
    fold = fold_ref[...]
    copies = [keep]
    for b in range(slot_count // LANES):
        out_ref[b] = fold_block(b, x_ref, dy_ref, fold)
        copies += start_all(
            [pltpu.make_async_copy(out_ref.at[b], send_hbm.at[b], out_sems.at[b])]
        )
    for copy in copies:
        copy.wait()


def hidden_units(x_ref, dy_ref, w_ref, hidden_ref, paired_ref):
    units = hidden_ref.shape[1]
    pre_gate = jnp.dot(x_ref[...], w_ref[0], preferred_element_type=jnp.float32)
    pre_up = jnp.dot(x_ref[...], w_ref[1], preferred_element_type=jnp.float32)
    hidden_grad = jnp.dot(dy_ref[...], w_ref[2], preferred_element_type=jnp.float32)
    gate_sig = jax.nn.sigmoid(pre_gate)
    gate_act = pre_gate * gate_sig
    hidden_ref[...] = (gate_act * pre_up).astype(jnp.bfloat16)
    gate_pre = hidden_grad * pre_up * gate_sig * (1.0 + pre_gate * (1.0 - gate_sig))
    paired_ref[:, :units] = gate_pre.astype(jnp.bfloat16)
    paired_ref[:, units:] = (hidden_grad * gate_act).astype(jnp.bfloat16)


def expert_kernel(
    recv_ref, ahead_hbm, back_hbm, unfold_hbm, fold_hbm,
    send_ref,
    ahead_ref, back_ref, unfold_ref, fold_ref,
    x_ref, dy_ref, hidden_ref, paired_ref, y_ref, dx_ref,
    load_sems,
):
    blocks = recv_ref.shape[0]
    feature_dim = x_ref.shape[1]
    units = hidden_ref.shape[1]
    pairs = [(unfold_hbm, unfold_ref)]
    pairs += [(ahead_hbm.at[i], ahead_ref.at[i]) for i in range(3)]
    pairs += [(back_hbm, back_ref), (fold_hbm, fold_ref)]
    loads = [
        pltpu.make_async_copy(src, dst, load_sems.at[i]) for i, (src, dst) in enumerate(pairs)
    ]
    loads[0].start()
    start_all(loads[1:])
    loads[0].wait()
    unfold = unfold_ref[...]
    for b in range(blocks):
        unfold_block(b, recv_ref[b], unfold, x_ref, dy_ref)
    for copy in loads[1:4]:
        copy.wait()
    hidden_units(x_ref, dy_ref, ahead_ref, hidden_ref, paired_ref)
    loads[4].wait()
    width = feature_dim // QUARTERS
    for q in range(QUARTERS):
        cols = slice(q * width, (q + 1) * width)
        y = jnp.dot(
            hidden_ref[...], back_ref[2 * units :, cols], preferred_element_type=jnp.float32
        )
        y_ref[:, cols] = y
        dx = jnp.dot(
            paired_ref[...], back_ref[: 2 * units, cols], preferred_element_type=jnp.float32
        )
        dx_ref[:, cols] = dx
    loads[5].wait()
    fold = fold_ref[...]
    for b in range(blocks):
        send_ref[b] = fold_block(b, y_ref, dx_ref, fold)


def grads_kernel(
    recv_hbm, w_hbm, unfold_hbm,
    terms_hbm,
    chunk_ref, w_ref, unfold_ref, x_ref, dy_ref, hidden_ref, paired_ref, terms_ref, load_sems, out_sems,
):
    units = hidden_ref.shape[1]
    pairs = [(recv_hbm, chunk_ref), (w_hbm, w_ref), (unfold_hbm, unfold_ref)]
    loads = start_all(
        [pltpu.make_async_copy(src, dst, load_sems.at[i]) for i, (src, dst) in enumerate(pairs)]
    )
    for copy in loads:
        copy.wait()
    for b in range(chunk_ref.shape[0]):
        unfold_block(b, chunk_ref[b], unfold_ref[...], x_ref, dy_ref)
    hidden_units(x_ref, dy_ref, w_ref, hidden_ref, paired_ref)
    width = x_ref.shape[1] // QUARTERS
    over_rows = (((0,), (0,)), ((), ()))
    copies = []
    for q in range(QUARTERS):
        cols = slice(q * width, (q + 1) * width)
        pair = lax.dot_general(
            x_ref[:, cols], paired_ref[...], over_rows, preferred_element_type=jnp.float32
        )
        terms_ref[cols, : 2 * units] = pair.astype(jnp.bfloat16)
        down = lax.dot_general(
            dy_ref[:, cols], hidden_ref[...], over_rows, preferred_element_type=jnp.float32
        )
        terms_ref[cols, 2 * units :] = down.astype(jnp.bfloat16)
        copies += start_all(
            [pltpu.make_async_copy(terms_ref.at[cols], terms_hbm.at[cols], out_sems.at[q])]
        )
    for copy in copies:
        copy.wait()


def finish_kernel(
    recv_ref, slots_ref, gates_ref, unfold_ref,
    outputs_hbm, grads_hbm,
    y_ref, dx_ref, outputs_ref, grads_ref, sems,
):
    blocks = recv_ref.shape[0]
    tok_rows, feature_dim = outputs_ref.shape
    slot_count = y_ref.shape[0]
    slot = lax.broadcasted_iota(jnp.int32, (tok_rows, slot_count), 1)
    hits = [slot == column(slots_ref[k : k + 1, :]) for k in range(2)]
    gates = [column(gates_ref[k : k + 1, :]) for k in range(2)]
    takers = [jnp.where(hit, 1.0, 0.0).astype(jnp.bfloat16) for hit in hits]
    both = jnp.where(hits[0] | hits[1], 1.0, 0.0).astype(jnp.bfloat16)
    unfold = unfold_ref[...]
    for b in range(blocks):
        unfold_block(b, recv_ref[b], unfold, y_ref, dx_ref)
    width = feature_dim // QUARTERS
    copies = []
    for q in range(QUARTERS):
        cols = slice(q * width, (q + 1) * width)
        total = sum(
            gates[k] * jnp.dot(takers[k], y_ref[:, cols], preferred_element_type=jnp.float32)
            for k in range(2)
        )
        outputs_ref[:, cols] = total.astype(jnp.bfloat16)
        grad = jnp.dot(both, dx_ref[:, cols], preferred_element_type=jnp.float32)
        grads_ref[:, cols] = grad.astype(jnp.bfloat16)
        copies += start_all(
            [
                pltpu.make_async_copy(
                    outputs_ref.at[:, cols], outputs_hbm.at[:, cols], sems.at[2 * q]
                ),
                pltpu.make_async_copy(
                    grads_ref.at[:, cols], grads_hbm.at[:, cols], sems.at[2 * q + 1]
                ),
            ]
        )
    for copy in copies:
        copy.wait()


def exchange(chunks, ep_count):
    width = chunks.shape[-1]
    moved = lax.all_to_all(
        chunks.reshape(ep_count, CHUNK, width), "ep", split_axis=0, concat_axis=0, tiled=True
    )
    return moved.reshape(chunks.shape)


def dp_partner(value, mask):
    pairs = [(source, source ^ mask) for source in range(lax.axis_size("dp"))]
    return lax.ppermute(value, "dp", pairs)


def body(tokens, cotangent, experts, gates, weights, swap_flags):
    ep_count = lax.axis_size("ep")
    half_ep = ep_count // 2
    tok_rows, feature_dim = tokens.shape
    slot_count = ep_count * CAP
    blocks = ep_count // GROUP
    units = weights.shape[3]
    width = feature_dim // QUARTERS
    my_index = lax.axis_index("ep")
    bf16 = jnp.bfloat16
    vmem = pl.BlockSpec(memory_space=pltpu.VMEM)
    hbm = pl.BlockSpec(memory_space=pltpu.HBM)
    dma = pltpu.SemaphoreType.DMA
    unfold = unfold_matrix()
    fold = jnp.asarray(unfold.T, bf16)
    unfold = jnp.asarray(unfold, bf16)
    chunks_shape = jax.ShapeDtypeStruct((blocks, BLOCK, width), bf16)
    rows_shape = jax.ShapeDtypeStruct((slot_count, feature_dim), bf16)
    tok_shape = jax.ShapeDtypeStruct((tok_rows, feature_dim), bf16)
    hidden_shape = jax.ShapeDtypeStruct((slot_count, units), bf16)
    paired_shape = jax.ShapeDtypeStruct((slot_count, 2 * units), bf16)
    slots_shape = jax.ShapeDtypeStruct((2, tok_rows), jnp.int32)

    wide_vmem = pltpu.VMEM(rows_shape.shape, jnp.float32)
    fold_vmem = pltpu.VMEM(fold.shape, bf16)

    def scratch(shape):
        return pltpu.VMEM(shape.shape, shape.dtype)

    gate_rows = gates.T
    send, slots = pl.pallas_call(
        prep_kernel,
        out_shape=(chunks_shape, slots_shape),
        in_specs=[hbm] * 6,
        out_specs=(hbm, hbm),
        scratch_shapes=[
            scratch(tok_shape),
            scratch(tok_shape),
            scratch(slots_shape),
            pltpu.VMEM((2, tok_rows), jnp.float32),
            pltpu.VMEM((1, half_ep), jnp.int32),
            fold_vmem,
            scratch(slots_shape),
            wide_vmem,
            wide_vmem,
            scratch(chunks_shape),
            dma((6,)),
            dma((blocks,)),
            dma,
        ],
        compiler_params=pltpu.CompilerParams(vmem_limit_bytes=VMEM_MIB * MIB),
        name="prep",
    )(tokens, cotangent, experts.T, gate_rows, swap_flags.reshape(1, half_ep), fold)

    pair_lanes = jnp.arange(half_ep, dtype=jnp.int32)
    my_flag = jnp.sum(jnp.where(pair_lanes == my_index % half_ep, swap_flags, 0)) > 0
    own_weights = weights[0]
    swap_pairs = [(source, source ^ half_ep) for source in range(ep_count)]
    partner = lax.ppermute(own_weights, "ep", swap_pairs)
    own_weights = jnp.where(my_flag, partner, own_weights)
    dp_count = lax.axis_size("dp")
    my_dp = lax.axis_index("dp")
    shard_rows = feature_dim // dp_count
    full_weights = jnp.zeros((3, feature_dim, units), bf16)
    for mask in range(dp_count):
        shard = own_weights if mask == 0 else dp_partner(own_weights, mask)
        start = (my_dp ^ mask) * shard_rows
        full_weights = lax.dynamic_update_slice_in_dim(full_weights, shard, start, axis=1)
    back = full_weights.transpose(0, 2, 1).reshape(3 * units, feature_dim)

    recv = exchange(send, ep_count)

    send_back = pl.pallas_call(
        expert_kernel,
        out_shape=chunks_shape,
        in_specs=[vmem] + [hbm] * 4,
        out_specs=vmem,
        scratch_shapes=[
            pltpu.VMEM((3, feature_dim, units), bf16),
            pltpu.VMEM((3 * units, feature_dim), bf16),
            fold_vmem,
            fold_vmem,
            scratch(rows_shape),
            scratch(rows_shape),
            scratch(hidden_shape),
            scratch(paired_shape),
            wide_vmem,
            wide_vmem,
            dma((6,)),
        ],
        compiler_params=pltpu.CompilerParams(vmem_limit_bytes=EXPERT_MIB * MIB),
        name="expert",
    )(recv, full_weights, back, unfold, fold)

    recv_back = exchange(send_back, ep_count)

    terms_shape = jax.ShapeDtypeStruct((feature_dim, 3 * units), bf16)
    terms = pl.pallas_call(
        grads_kernel,
        out_shape=terms_shape,
        in_specs=[hbm] * 3,
        out_specs=hbm,
        scratch_shapes=[
            scratch(chunks_shape),
            pltpu.VMEM((3, feature_dim, units), bf16),
            fold_vmem,
            scratch(rows_shape),
            scratch(rows_shape),
            scratch(hidden_shape),
            scratch(paired_shape),
            scratch(terms_shape),
            dma((3,)),
            dma((QUARTERS,)),
        ],
        compiler_params=pltpu.CompilerParams(vmem_limit_bytes=GRADS_MIB * MIB),
        name="grads",
    )(recv, full_weights, unfold)
    total = jnp.zeros((shard_rows, 3 * units), jnp.float32)
    for mask in range(dp_count):
        start = (my_dp ^ mask) * shard_rows
        shard = lax.dynamic_slice_in_dim(terms, start, shard_rows, 0)
        total += (shard if mask == 0 else dp_partner(shard, mask)).astype(jnp.float32)
    mine = total.astype(bf16)
    weight_grads = jnp.stack(
        [mine[:, :units], mine[:, units : 2 * units], mine[:, 2 * units :]]
    )[None]

    outputs, input_grads = pl.pallas_call(
        finish_kernel,
        out_shape=(tok_shape, tok_shape),
        in_specs=[vmem] * 4,
        out_specs=(hbm, hbm),
        scratch_shapes=[
            scratch(rows_shape),
            scratch(rows_shape),
            scratch(tok_shape),
            scratch(tok_shape),
            dma((2 * QUARTERS,)),
        ],
        compiler_params=pltpu.CompilerParams(vmem_limit_bytes=40 * MIB),
        name="finish",
    )(recv_back, slots, gate_rows, unfold)
    return (outputs, input_grads, weight_grads)


def solution(mesh):
    return jax.shard_map(
        body,
        mesh=mesh,
        in_specs=(
            P(("ep", "dp"), None),
            P(("ep", "dp"), None),
            P(("ep", "dp"), None),
            P(("ep", "dp"), None),
            P("ep", None, "dp", None),
            P(),
        ),
        out_specs=(P(("ep", "dp"), None), P(("ep", "dp"), None), P("ep", None, "dp", None)),
        check_vma=False,
    )
```
